512 devices in a mesh: path: 64 (over x, z, core), shard: 8 (over y).
Axes of the slice: x: 4, y: 8, z: 8, core: 2. Of those that a mesh axis runs over, the one named last changes fastest.
Arguments:
- deltas: bfloat16 [64, 128, 4096], P('path', 'shard'), may hold values from -96 to 96
- momentum: float32 [16, 128, 4096], P(None, 'shard', 'path'), may hold values from -4 to 4
- path_module: int32 [64], replicated, may hold values from 0 to 15, as said below
Outputs:
- path_update: bfloat16 [64, 128, 4096], P('path', 'shard')
- new_momentum: float32 [16, 128, 4096], P(None, 'shard', 'path')
The draws below stay inside these ranges and needn't reach their ends.
Inputs may be any that keep to these rules, and one draw needn't show every extreme that they name: `path_module`: every module is used by at least one and at most seven paths.
All inputs are finite; a program needn't handle non-finite values.
Results may differ from the reference program's by a relative error of at most 0.0004.
Values may be sent and summed in bfloat16 or wider, within the bound.
No kernel may reach another device: no remote copies, remote signals or barrier semaphores. Data moves between devices by JAX's collectives and lax.ppermute only.
A program may use at most 64 MiB of HBM per device.

```python
import jax
import jax.numpy as jnp
from jax import lax

D = 4096
MODULES = 16
ROWS = 128
PATHS = 64


def draw_deltas(key, part):
    row_pos = jnp.arange(ROWS, dtype=jnp.float32) / ROWS
    col_pos = jnp.arange(D, dtype=jnp.float32) / D
    ramp = (1.0 + row_pos)[:, None] * (1.0 + col_pos)[None, :]
    log_scale = jax.random.uniform(jax.random.fold_in(key, 7), (PATHS, 1, 1), jnp.float32, -1.3862944, 1.3862944)
    path_scale = jnp.exp(log_scale)
    values = jnp.clip(jax.random.normal(key, (PATHS, ROWS, D), jnp.float32), -6.0, 6.0) * path_scale
    return (values * ramp).astype(jnp.bfloat16)


def draw_path_module(key, part):
    first = jax.random.permutation(jax.random.fold_in(key, 1), MODULES).astype(jnp.int32)
    repeated = jnp.tile(jnp.arange(MODULES, dtype=jnp.int32), 6)
    others = jax.random.permutation(jax.random.fold_in(key, 2), repeated)[:PATHS - MODULES].astype(jnp.int32)
    labels = jnp.concatenate([first, others])
    return jax.random.permutation(jax.random.fold_in(key, 3), labels).astype(jnp.int32)


def shard_levels(stream_key, dims, cuts, low, largest):
    factor_of, own = 1.0, jax.random.fold_in(stream_key, 6)
    for axis_at, shards_of in cuts:
        steps = jnp.exp(jax.random.uniform(jax.random.fold_in(own, axis_at), (shards_of,), jnp.float32, low / len(cuts), largest / len(cuts)))
        factor_of = factor_of * jnp.repeat(steps, dims[axis_at] // shards_of).reshape([-1 if axis == axis_at else 1 for axis in range(len(dims))])
    return factor_of


def normal_values(rng, extent, deviation, bound, pieces=(), kind=jnp.bfloat16):
    entries = jax.random.normal(rng, extent, jnp.float32) * deviation
    if len(pieces) > 0:
        entries = shard_levels(rng, extent, pieces, -0.22, 0.18) * entries
    return jnp.clip(entries, min=-bound, max=bound).astype(kind)


def setup_inputs(seed: int = 0) -> dict:
    keys = jax.random.split(jax.random.key(seed), 4)
    deltas = draw_deltas(jax.random.fold_in(keys[3], 71), 0)
    momentum = normal_values(keys[1], (MODULES, ROWS, D), 0.25, 4.0, ((1, 8), (2, 64)), jnp.float32)
    path_module = draw_path_module(jax.random.fold_in(keys[3], 71), 0)
    return dict(deltas=deltas, momentum=momentum, path_module=path_module)


outer_rate = 0.7
momentum_rate = 0.9
clip_ratio = 2.0

def reference(deltas, momentum, path_module):
    onehot = (path_module[:, None] == jnp.arange(MODULES, dtype=jnp.int32)[None, :]).astype(jnp.float32)
    counts = lax.optimization_barrier(jnp.sum(onehot, axis=0))
    totals = jnp.einsum('pm,prc->mrc', onehot, deltas.astype(jnp.float32), precision=lax.Precision.HIGHEST)
    outer_grad = totals / counts[:, None, None]
    norm_squares = lax.optimization_barrier(jnp.sum(outer_grad * outer_grad, axis=(1, 2)))
    limit = clip_ratio * jnp.sqrt(jnp.float32(ROWS * D))
    shrink = jnp.minimum(1.0, limit / jnp.sqrt(norm_squares + 1e-06))
    clipped = outer_grad * shrink[:, None, None]
    new_momentum = momentum_rate * momentum + clipped
    outer_step = (outer_rate * (clipped + momentum_rate * new_momentum)).astype(jnp.bfloat16)
    path_update = jnp.einsum('pm,mrc->prc', onehot, outer_step.astype(jnp.float32), precision=lax.Precision.HIGHEST).astype(jnp.bfloat16)
    return (path_update, new_momentum)
```

```python
import jax
import jax.numpy as jnp
from jax import lax
from jax.experimental import pallas as pl
from jax.experimental.pallas import tpu as pltpu
from jax.sharding import Mesh
from jax.sharding import PartitionSpec as P

PATH = ("path_0", "path_1", "path_2")
TILES = ("path_2", "path_0", "path_1")

outer_rate = 0.7
momentum_rate = 0.9
clip_ratio = 2.0

GRAD, MOMENTUM, SQUARES, CHUNK = 0, 8, 16, 17
KERNEL_BYTES = 4 << 20
VMEM = pl.BlockSpec(memory_space=pltpu.VMEM)
SMEM = pl.BlockSpec(memory_space=pltpu.SMEM)


def path_of(peer, chips):
    return (peer % chips) * 2 + peer // chips


def lanes():
    return lax.broadcasted_iota(jnp.int32, (8, 128), 1)


def gather_kernel(module_ref, column_ref, momentum_ref, chunk_ref, grad_ref, *scratch):
    *sums, packed, count = scratch
    peers, modules = column_ref.shape[0], grad_ref.shape[0]
    chips = peers // 2
    for total in sums:
        total[...] = jnp.zeros_like(total)
    for m in range(modules):
        count[m] = 0
    for q in range(peers):
        m = module_ref[path_of(q, chips)]
        total = sums[q % len(sums)]
        total[m] += column_ref[q].astype(jnp.float32)
        count[m] += 1
    first_core = lax.axis_index("path_2") == 0
    for m in range(modules):
        total = sums[0][m]
        for more in sums[1:]:
            total += more[m]
        grad_ref[m] = total / count[m].astype(jnp.float32)
        top, bottom = momentum_ref[m, 0:8, :], momentum_ref[m, 8:16, :]
        packed[m] = jnp.concatenate(
            [jnp.where(first_core, top, bottom), jnp.where(first_core, bottom, top)], axis=1
        )
    grad = grad_ref[...]
    squares = jnp.sum(jnp.sum(grad * grad, axis=1), axis=1, keepdims=True)
    row = lax.broadcasted_iota(jnp.int32, (modules, 128), 0)
    lane = lax.broadcasted_iota(jnp.int32, (modules, 128), 1)
    squares = jnp.sum(jnp.where(row == lane, squares, 0.0), axis=0, keepdims=True)
    for q in range(peers):
        m = module_ref[path_of(q, chips)]
        start = q * CHUNK
        chunk_ref[start + GRAD : start + MOMENTUM, :] = grad_ref[m]
        chunk_ref[start + MOMENTUM : start + SQUARES, :] = packed[m]
        chunk_ref[start + SQUARES : start + CHUNK, :] = squares


def step_kernel(limit, module_ref, squares_ref, chunk_ref, mine_ref, other_ref, momentum_ref, update_ref, new_ref):
    peers, modules = update_ref.shape[0], mine_ref.shape[0]
    chips = peers // 2
    core = lax.axis_index("path_2")
    chip = lax.axis_index("path_0") * lax.axis_size("path_1") + lax.axis_index("path_1")
    norm_squares = jnp.sum(squares_ref[...], axis=0, keepdims=True)
    shrink = jnp.minimum(1.0, limit / jnp.sqrt(norm_squares + 1e-06))
    lane = lax.broadcasted_iota(jnp.int32, (1, 128), 1)

    def of_module(m):
        return jnp.sum(jnp.where(lane == m, shrink, 0.0), axis=1, keepdims=True)

    own = jnp.broadcast_to(of_module(module_ref[chip * 2 + core]), (8, 128))
    left = lanes() < 64
    for q in range(peers):
        half, at = q // chips, q % chips
        start = q * CHUNK
        one = chunk_ref[at * CHUNK + MOMENTUM : at * CHUNK + SQUARES, :]
        two = chunk_ref[(chips + at) * CHUNK + MOMENTUM : (chips + at) * CHUNK + SQUARES, :]
        if half == 0:
            momentum = jnp.where(left, one, two)
        else:
            momentum = pltpu.roll(jnp.where(left, two, one), 64, 1)
        clipped = chunk_ref[start + GRAD : start + MOMENTUM, :] * own
        new_momentum = momentum_rate * momentum + clipped
        step = outer_rate * (clipped + momentum_rate * new_momentum)
        update_ref[q] = step.astype(jnp.bfloat16)
    first_core = core == 0
    for m in range(modules):
        k = jnp.broadcast_to(of_module(m), (8, 128))
        for half in range(2):
            grad = jnp.where(core == half, mine_ref[m], other_ref[m]) * k
            grad = jnp.where(first_core, grad, pltpu.roll(grad, 64, 1))
            rows = slice(half * 8, half * 8 + 8)
            new_ref[m, rows, :] = momentum_rate * momentum_ref[m, rows, :] + grad[:, 0:64]


def local(deltas, momentum, path_module):
    modules, rows, _ = momentum.shape
    columns = deltas.shape[2]
    peers = lax.axis_size(PATH)
    shards = lax.axis_size("shard")
    tiles = deltas.reshape(2, 8, peers // 2, 128).transpose(0, 2, 1, 3).reshape(peers, 8, 128)
    column_tiles = lax.all_to_all(tiles, TILES, 0, 0, tiled=True)
    chunks, grad = pl.pallas_call(
        gather_kernel,
        out_shape=(
            jax.ShapeDtypeStruct((peers * CHUNK, 128), jnp.float32),
            jax.ShapeDtypeStruct((modules, 8, 128), jnp.float32),
        ),
        in_specs=[SMEM, VMEM, VMEM],
        out_specs=(VMEM, VMEM),
        scratch_shapes=[pltpu.VMEM((modules, 8, 128), jnp.float32)] * 5
        + [pltpu.SMEM((modules,), jnp.int32)],
        compiler_params=pltpu.CompilerParams(vmem_limit_bytes=KERNEL_BYTES),
        name="gather_modules",
    )(path_module, column_tiles, momentum)
    chunks = lax.all_to_all(chunks.reshape(peers, CHUNK, 1, 128), TILES, 0, 0, tiled=True)
    other = lax.ppermute(grad, "path_2", [(0, 1), (1, 0)])
    squares = jnp.sum(chunks[:, SQUARES], axis=0)
    squares = lax.all_to_all(
        jnp.broadcast_to(squares, (shards, 1, 128)), "shard", 0, 0, tiled=True
    )
    limit = clip_ratio * float(rows * shards * columns) ** 0.5
    update, new_momentum = pl.pallas_call(
        lambda *refs: step_kernel(limit, *refs),
        out_shape=(
            jax.ShapeDtypeStruct((peers, 8, 128), jnp.bfloat16),
            jax.ShapeDtypeStruct(momentum.shape, jnp.float32),
        ),
        in_specs=[SMEM, VMEM, VMEM, VMEM, VMEM, VMEM],
        out_specs=(VMEM, VMEM),
        compiler_params=pltpu.CompilerParams(vmem_limit_bytes=KERNEL_BYTES),
        name="step",
    )(
        path_module,
        squares.reshape(shards, 128),
        chunks.reshape(peers * CHUNK, 128),
        grad,
        other,
        momentum,
    )
    update = update.reshape(2, peers // 2, 8, 128).transpose(0, 2, 1, 3).reshape(deltas.shape)
    return (update, new_momentum)


def solution(mesh):
    finer = Mesh(
        mesh.devices.reshape(4, 8, 2, mesh.shape["shard"]), ("path_0", "path_1", "path_2", "shard")
    )
    in_specs = (P(PATH, "shard", None), P(None, "shard", PATH), P())
    out_specs = (P(PATH, "shard", None), P(None, "shard", PATH))
    return jax.shard_map(local, mesh=finer, in_specs=in_specs, out_specs=out_specs, check_vma=False)
```

```python
import jax
import jax.numpy as jnp
from jax import lax
from jax.experimental import pallas as pl
from jax.experimental.pallas import tpu as pltpu
from jax.sharding import Mesh
from jax.sharding import PartitionSpec as P

PATH = ("path_0", "path_1", "path_2")
TILES = ("path_2", "path_0", "path_1")

outer_rate = 0.7
momentum_rate = 0.9
clip_ratio = 2.0

GRAD, MOMENTUM, SQUARES, CHUNK = 0, 8, 16, 17
KERNEL_BYTES = 4 << 20
VMEM = pl.BlockSpec(memory_space=pltpu.VMEM)
SMEM = pl.BlockSpec(memory_space=pltpu.SMEM)
HBM = pl.BlockSpec(memory_space=pl.ANY)
PIECES = 4


def path_of(peer, chips):
    return (peer % chips) * 2 + peer // chips


def kernel(body, name, **kwargs):
    params = pltpu.CompilerParams(vmem_limit_bytes=KERNEL_BYTES)
    return pl.pallas_call(body, name=name, compiler_params=params, **kwargs)


def momentum_kernel(module_ref, momentum_ref, chunk_ref, packed):
    first_core = lax.axis_index("path_2") == 0
    for m in range(momentum_ref.shape[0]):
        top, bottom = momentum_ref[m, 0:8, :], momentum_ref[m, 8:16, :]
        packed[m] = jnp.concatenate(
            [jnp.where(first_core, top, bottom), jnp.where(first_core, bottom, top)], axis=1
        )
    peers = chunk_ref.shape[0] // CHUNK
    for q in range(peers):
        start = q * CHUNK
        m = module_ref[path_of(q, peers // 2)]
        chunk_ref[start + MOMENTUM : start + SQUARES, :] = packed[m]


def gather_kernel(module_ref, column_ref, _, chunk_ref, chunk_out, grad_ref, *scratch):
    *sums, count, sems = scratch
    peers, modules = column_ref.shape[0], grad_ref.shape[0]
    chips = peers // 2
    for total in sums:
        total[...] = jnp.zeros_like(total)
    for m in range(modules):
        count[m] = 0
    for q in range(peers):
        m = module_ref[path_of(q, chips)]
        total = sums[q % len(sums)]
        total[m] += column_ref[q].astype(jnp.float32)
        count[m] += 1
    for m in range(modules):
        total = sums[0][m]
        for more in sums[1:]:
            total += more[m]
        grad_ref[m] = total / count[m].astype(jnp.float32)
    grad = grad_ref[...]
    squares = jnp.sum(jnp.sum(grad * grad, axis=1), axis=1, keepdims=True)
    row = lax.broadcasted_iota(jnp.int32, (modules, 128), 0)
    lane = lax.broadcasted_iota(jnp.int32, (modules, 128), 1)
    squares = jnp.sum(jnp.where(row == lane, squares, 0.0), axis=0, keepdims=True)
    copies = []
    for q in range(peers):
        m = module_ref[path_of(q, chips)]
        start = q * CHUNK
        chunk_ref[start + GRAD : start + MOMENTUM, :] = grad_ref[m]
        chunk_ref[start + SQUARES : start + CHUNK, :] = squares
        if (q + 1) % (peers // PIECES) == 0:
            piece = pl.ds(len(copies) * (peers // PIECES) * CHUNK, (peers // PIECES) * CHUNK)
            sem = sems.at[len(copies)]
            copies.append(pltpu.make_async_copy(chunk_ref.at[piece], chunk_out.at[piece], sem))
            copies[-1].start()
    for copy in copies:
        copy.wait()


def assemble_kernel(
    module_ref, chunk_ref, mine_ref, other_ref, grad_ref, decay_ref, own_grad_ref, own_ref
):
    peers, modules = grad_ref.shape[0], mine_ref.shape[0]
    chips = peers // 2
    core = lax.axis_index("path_2")
    chip = lax.axis_index("path_0") * lax.axis_size("path_1") + lax.axis_index("path_1")
    left = lax.broadcasted_iota(jnp.int32, (8, 128), 1) < 64
    for at in range(chips):
        first, second = at * CHUNK, (chips + at) * CHUNK
        grad_ref[at] = chunk_ref[first + GRAD : first + MOMENTUM, :]
        grad_ref[chips + at] = chunk_ref[second + GRAD : second + MOMENTUM, :]
        one = chunk_ref[first + MOMENTUM : first + SQUARES, :]
        two = chunk_ref[second + MOMENTUM : second + SQUARES, :]
        decay_ref[at] = momentum_rate * jnp.where(left, one, two)
        decay_ref[chips + at] = momentum_rate * pltpu.roll(jnp.where(left, two, one), 64, 1)
    for m in range(modules):
        for half in range(2):
            grad = jnp.where(core == half, mine_ref[m], other_ref[m])
            grad = jnp.where(core == 0, grad, pltpu.roll(grad, 64, 1))
            own_grad_ref[m, half * 8 : half * 8 + 8, :] = grad[:, 0:64]
    lane = lax.broadcasted_iota(jnp.int32, (1, 128), 1)
    own_ref[...] = (lane == module_ref[chip * 2 + core]).astype(jnp.float32)


def step_kernel(
    limit, squares_ref, grad_ref, decay_ref, own_grad_ref, own_ref, momentum_ref,
    update_out, new_out, update, new, sems,
):
    peers, modules = update.shape[0], new.shape[0]
    norm_squares = jnp.sum(squares_ref[...], axis=0, keepdims=True)
    shrink = jnp.minimum(1.0, limit / jnp.sqrt(norm_squares + 1e-06))
    own = jnp.sum(shrink * own_ref[...], axis=1, keepdims=True)
    each = peers // PIECES
    copies = []
    for piece in range(PIECES):
        tiles = slice(piece * each, (piece + 1) * each)
        clipped = grad_ref[tiles] * own.reshape(1, 1, 1)
        step = outer_rate * (clipped + momentum_rate * (decay_ref[tiles] + clipped))
        update[tiles] = step.astype(jnp.bfloat16)
        copies.append(pltpu.make_async_copy(update.at[tiles], update_out.at[tiles], sems.at[piece]))
        copies[-1].start()
    lane = lax.broadcasted_iota(jnp.int32, (1, 128), 1)
    for m in range(modules):
        k = jnp.sum(jnp.where(lane == m, shrink, 0.0), axis=1, keepdims=True)
        new[m] = momentum_rate * momentum_ref[m] + own_grad_ref[m] * k
    copies.append(pltpu.make_async_copy(new, new_out, sems.at[PIECES]))
    copies[-1].start()
    for copy in copies:
        copy.wait()


def local(deltas, momentum, path_module):
    modules, rows, width = momentum.shape
    columns = deltas.shape[2]
    peers = lax.axis_size(PATH)
    shards = lax.axis_size("shard")
    shape = jax.ShapeDtypeStruct
    tiles = deltas.reshape(2, 8, peers // 2, 128).transpose(0, 2, 1, 3).reshape(peers, 8, 128)
    column_tiles = lax.all_to_all(tiles, TILES, 0, 0, tiled=True)
    chunks = kernel(
        momentum_kernel,
        "pack_momentum",
        out_shape=shape((peers * CHUNK, 128), jnp.float32),
        in_specs=[SMEM, VMEM],
        out_specs=VMEM,
        scratch_shapes=[pltpu.VMEM((modules, 8, 128), jnp.float32)],
    )(path_module, momentum)
    _, chunks, grad = kernel(
        gather_kernel,
        "gather_modules",
        out_shape=(
            shape((peers * CHUNK, 128), jnp.float32),
            shape((peers * CHUNK, 128), jnp.float32),
            shape((modules, 8, 128), jnp.float32),
        ),
        in_specs=[SMEM, VMEM, VMEM],
        out_specs=(VMEM, HBM, VMEM),
        input_output_aliases={2: 0},
        scratch_shapes=[pltpu.VMEM((modules, 8, 128), jnp.float32)] * 4
        + [pltpu.SMEM((modules,), jnp.int32), pltpu.SemaphoreType.DMA((PIECES,))],
    )(path_module, column_tiles, chunks)
    chunks = lax.all_to_all(chunks.reshape(peers, CHUNK, 1, 128), TILES, 0, 0, tiled=True)
    other = lax.ppermute(grad, "path_2", [(0, 1), (1, 0)])
    chunks, other = lax.optimization_barrier((chunks, other))
    squares = jnp.sum(chunks[:, SQUARES], axis=0)
    squares = lax.all_to_all(
        jnp.broadcast_to(squares, (shards, 1, 128)), "shard", 0, 0, tiled=True
    )
    path_tiles = shape((peers, 8, 128), jnp.float32)
    assembled = kernel(
        assemble_kernel,
        "assemble",
        out_shape=(
            path_tiles,
            path_tiles,
            shape(momentum.shape, jnp.float32),
            shape((1, 128), jnp.float32),
        ),
        in_specs=[SMEM, VMEM, VMEM, VMEM],
        out_specs=(VMEM,) * 4,
    )(path_module, chunks.reshape(peers * CHUNK, 128), grad, other)
    limit = clip_ratio * float(rows * shards * columns) ** 0.5
    update, new_momentum = kernel(
        lambda *refs: step_kernel(limit, *refs),
        "step",
        out_shape=(
            shape((peers, 8, 128), jnp.bfloat16),
            shape(momentum.shape, jnp.float32),
        ),
        in_specs=[VMEM] * 6,
        out_specs=(HBM, HBM),
        scratch_shapes=[
            pltpu.VMEM((peers, 8, 128), jnp.bfloat16),
            pltpu.VMEM(momentum.shape, jnp.float32),
            pltpu.SemaphoreType.DMA((PIECES + 1,)),
        ],
    )(squares.reshape(shards, 128), *assembled, momentum)
    update = update.reshape(2, peers // 2, 8, 128).transpose(0, 2, 1, 3).reshape(deltas.shape)
    return (update, new_momentum)


def solution(mesh):
    finer = Mesh(
        mesh.devices.reshape(4, 8, 2, mesh.shape["shard"]), ("path_0", "path_1", "path_2", "shard")
    )
    in_specs = (P(PATH, "shard", None), P(None, "shard", PATH), P())
    out_specs = (P(PATH, "shard", None), P(None, "shard", PATH))
    return jax.shard_map(local, mesh=finer, in_specs=in_specs, out_specs=out_specs, check_vma=False)
```

```python
import jax
import jax.numpy as jnp
from jax import lax
from jax.experimental import pallas as pl
from jax.experimental.pallas import tpu as pltpu
from jax.sharding import Mesh
from jax.sharding import PartitionSpec as P

PATH = ("path_0", "path_1", "path_2")
TILES = ("path_2", "path_0", "path_1")

outer_rate = 0.7
momentum_rate = 0.9
clip_ratio = 2.0

LOW, SQUARES, CHUNK = 8, 10, 11
GRAD_BITS = 23
MOMENTUM_SCALE = 8191.0
SQUARES_SCALE = 128.0
FOLD = momentum_rate * momentum_rate / (1.0 + momentum_rate)
KERNEL_BYTES = 4 << 20
VMEM = pl.BlockSpec(memory_space=pltpu.VMEM)
SMEM = pl.BlockSpec(memory_space=pltpu.SMEM)
HBM = pl.BlockSpec(memory_space=pl.ANY)
PIECES = 4


def path_of(peer, chips):
    return (peer % chips) * 2 + peer // chips


def kernel(body, name, **kwargs):
    params = pltpu.CompilerParams(vmem_limit_bytes=KERNEL_BYTES)
    return pl.pallas_call(body, name=name, compiler_params=params, **kwargs)


def nearest(x):
    return jnp.floor(x + 0.5).astype(jnp.int32)


def momentum_kernel(module_ref, mine_ref, other_ref, chunk_ref, high_ref, fold_ref, low):
    first_core = lax.axis_index("path_2") == 0
    row = lax.broadcasted_iota(jnp.int32, (8, 128), 0)
    for m in range(mine_ref.shape[0]):
        mine = jnp.where(first_core, mine_ref[m, 0:8, :], mine_ref[m, 8:16, :])
        other = jnp.where(first_core, other_ref[m, 0:8, :], other_ref[m, 8:16, :])
        momentum = jnp.concatenate(
            [jnp.where(first_core, mine, other), jnp.where(first_core, other, mine)], axis=1
        )
        whole = nearest(momentum * MOMENTUM_SCALE)
        fold_ref[m] = FOLD * (momentum - whole.astype(jnp.float32) * (1.0 / MOMENTUM_SCALE))
        whole += 32768
        high_ref[m] = whole >> 8
        word = (whole & 255) << ((row & 3) * 8)
        word = word | pltpu.roll(word, 7, 0)
        word = word | pltpu.roll(word, 6, 0)
        low[m, 0:1, :] = word[0:1, :]
        low[m, 1:2, :] = word[4:5, :]
    peers = chunk_ref.shape[0] // CHUNK
    for q in range(peers):
        start = q * CHUNK
        m = module_ref[path_of(q, peers // 2)]
        chunk_ref[start + LOW : start + SQUARES, :] = low[m, 0:2, :]


def gather_kernel(
    module_ref, column_ref, high_ref, fold_ref, _, chunk_ref, chunk_out, grad_ref, *scratch
):
    *sums, words, count, sems = scratch
    peers, modules = column_ref.shape[0], grad_ref.shape[0]
    chips = peers // 2
    for total in sums:
        total[...] = jnp.zeros_like(total)
    for m in range(modules):
        count[m] = 0
    for q in range(peers):
        m = module_ref[path_of(q, chips)]
        total = sums[q % len(sums)]
        total[m] += column_ref[q].astype(jnp.float32)
        count[m] += 1
    for m in range(modules):
        total = sums[0][m]
        for more in sums[1:]:
            total += more[m]
        grad_ref[m] = total / count[m].astype(jnp.float32)
    grad = grad_ref[...]
    squares = jnp.sum(jnp.sum(grad * grad, axis=1), axis=1, keepdims=True)
    largest = jnp.max(jnp.max(jnp.abs(grad + fold_ref[...]), axis=1), axis=1, keepdims=True)
    power = jnp.ceil(jnp.log2(jnp.maximum(largest, 1e-30)))
    scale = jnp.exp2(GRAD_BITS - power)
    limit = 2.0**GRAD_BITS - 1.0
    for m in range(modules):
        exact = (grad_ref[m] + fold_ref[m]) * scale[m : m + 1, :]
        words[m] = (nearest(jnp.clip(exact, -limit, limit)) << 8) | high_ref[m]
    row = lax.broadcasted_iota(jnp.int32, (modules, 128), 0)
    lane = lax.broadcasted_iota(jnp.int32, (modules, 128), 1)
    tail = jnp.where(row == lane, squares * SQUARES_SCALE, 0.0)
    tail = jnp.where(row + modules == lane, power, tail)
    tail = nearest(jnp.sum(tail, axis=0, keepdims=True))
    copies = []
    for q in range(peers):
        m = module_ref[path_of(q, chips)]
        start = q * CHUNK
        chunk_ref[start : start + LOW, :] = words[m]
        chunk_ref[start + SQUARES : start + CHUNK, :] = tail
        if (q + 1) % (peers // PIECES) == 0:
            piece = pl.ds(len(copies) * (peers // PIECES) * CHUNK, (peers // PIECES) * CHUNK)
            sem = sems.at[len(copies)]
            copies.append(pltpu.make_async_copy(chunk_ref.at[piece], chunk_out.at[piece], sem))
            copies[-1].start()
    for copy in copies:
        copy.wait()


def assemble_kernel(
    module_ref, chunk_ref, mine_ref, other_ref, grad_ref, decay_ref, own_grad_ref, own_ref
):
    peers, modules = grad_ref.shape[0], mine_ref.shape[0]
    core = lax.axis_index("path_2")
    chip = lax.axis_index("path_0") * lax.axis_size("path_1") + lax.axis_index("path_1")
    module = module_ref[chip * 2 + core]
    tail = chunk_ref[pl.ds(SQUARES, peers, stride=CHUNK), :]
    lane = lax.broadcasted_iota(jnp.int32, (peers, 128), 1)
    power = jnp.where(lane == module + modules, tail, 0).astype(jnp.float32)
    power = jnp.sum(power, axis=1, keepdims=True)
    scale = jnp.broadcast_to(1.0 / jnp.exp2(GRAD_BITS - power), (peers, 128))
    row = lax.broadcasted_iota(jnp.int32, (8, 128), 0)
    shift = (row & 3) * 8
    for q in range(peers):
        start = q * CHUNK
        words = chunk_ref[start : start + LOW, :]
        grad_ref[q] = (words >> 8).astype(jnp.float32) * scale[q : q + 1, :]
        one, two = chunk_ref[start + LOW : start + LOW + 1, :], chunk_ref[start + LOW + 1 : start + SQUARES, :]
        low = (jnp.where(row < 4, one, two) >> shift) & 255
        whole = (((words & 255) << 8) | low) - 32768
        decay_ref[q] = whole.astype(jnp.float32) * (momentum_rate / MOMENTUM_SCALE)
    for m in range(modules):
        for half in range(2):
            grad = jnp.where(core == half, mine_ref[m], other_ref[m])
            grad = jnp.where(core == 0, grad, pltpu.roll(grad, 64, 1))
            own_grad_ref[m, half * 8 : half * 8 + 8, :] = grad[:, 0:64]
    own_ref[...] = (lane[0:1, :] == module).astype(jnp.float32)


def step_kernel(
    limit, squares_ref, grad_ref, decay_ref, own_grad_ref, own_ref, momentum_ref,
    update_out, new_out, update, new, sems,
):
    peers, modules = update.shape[0], new.shape[0]
    norm_squares = jnp.sum(squares_ref[...], axis=0, keepdims=True)
    shrink = jnp.minimum(1.0, limit / jnp.sqrt(norm_squares + 1e-06))
    own = jnp.sum(jnp.where(own_ref[...] > 0.0, shrink, 0.0), axis=1, keepdims=True)
    each = peers // PIECES
    copies = []
    for piece in range(PIECES):
        tiles = slice(piece * each, (piece + 1) * each)
        clipped = grad_ref[tiles] * own.reshape(1, 1, 1)
        step = outer_rate * (clipped + momentum_rate * (decay_ref[tiles] + clipped))
        update[tiles] = step.astype(jnp.bfloat16)
        copies.append(pltpu.make_async_copy(update.at[tiles], update_out.at[tiles], sems.at[piece]))
        copies[-1].start()
    lane = lax.broadcasted_iota(jnp.int32, (1, 128), 1)
    for m in range(modules):
        k = jnp.sum(jnp.where(lane == m, shrink, 0.0), axis=1, keepdims=True)
        new[m] = momentum_rate * momentum_ref[m] + own_grad_ref[m] * k
    copies.append(pltpu.make_async_copy(new, new_out, sems.at[PIECES]))
    copies[-1].start()
    for copy in copies:
        copy.wait()


def local(deltas, momentum, path_module):
    modules, rows, width = momentum.shape
    columns = deltas.shape[2]
    peers = lax.axis_size(PATH)
    shards = lax.axis_size("shard")
    shape = jax.ShapeDtypeStruct
    tiles = deltas.reshape(2, 8, peers // 2, 128).transpose(0, 2, 1, 3).reshape(peers, 8, 128)
    column_tiles = lax.all_to_all(tiles, TILES, 0, 0, tiled=True)
    other = lax.ppermute(momentum, "path_2", [(0, 1), (1, 0)])
    module_tiles = shape((modules, 8, 128), jnp.float32)
    chunk_rows = shape((peers * CHUNK, 128), jnp.int32)
    chunks, high, fold = kernel(
        momentum_kernel,
        "pack_momentum",
        out_shape=(chunk_rows, shape((modules, 8, 128), jnp.int32), module_tiles),
        in_specs=[SMEM, VMEM, VMEM],
        out_specs=(VMEM,) * 3,
        scratch_shapes=[pltpu.VMEM((modules, 8, 128), jnp.int32)],
    )(path_module, momentum, other)
    _, chunks, grad = kernel(
        gather_kernel,
        "gather_modules",
        out_shape=(chunk_rows, chunk_rows, module_tiles),
        in_specs=[SMEM, VMEM, VMEM, VMEM, VMEM],
        out_specs=(VMEM, HBM, VMEM),
        input_output_aliases={4: 0},
        scratch_shapes=[pltpu.VMEM((modules, 8, 128), jnp.float32)] * 4
        + [
            pltpu.VMEM((modules, 8, 128), jnp.int32),
            pltpu.SMEM((modules,), jnp.int32),
            pltpu.SemaphoreType.DMA((PIECES,)),
        ],
    )(path_module, column_tiles, high, fold, chunks)
    chunks = lax.all_to_all(chunks.reshape(peers, CHUNK, 1, 128), TILES, 0, 0, tiled=True)
    other = lax.ppermute(grad, "path_2", [(0, 1), (1, 0)])
    chunks, other = lax.optimization_barrier((chunks, other))
    squares = jnp.sum(chunks[:, SQUARES].astype(jnp.float32) * (1.0 / SQUARES_SCALE), axis=0)
    squares = lax.all_to_all(
        jnp.broadcast_to(squares, (shards, 1, 128)), "shard", 0, 0, tiled=True
    )
    path_tiles = shape((peers, 8, 128), jnp.float32)
    assembled = kernel(
        assemble_kernel,
        "assemble",
        out_shape=(
            path_tiles,
            path_tiles,
            shape(momentum.shape, jnp.float32),
            shape((1, 128), jnp.float32),
        ),
        in_specs=[SMEM, VMEM, VMEM, VMEM],
        out_specs=(VMEM,) * 4,
    )(path_module, chunks.reshape(peers * CHUNK, 128), grad, other)
    limit = clip_ratio * float(rows * shards * columns) ** 0.5
    update, new_momentum = kernel(
        lambda *refs: step_kernel(limit, *refs),
        "step",
        out_shape=(
            shape((peers, 8, 128), jnp.bfloat16),
            shape(momentum.shape, jnp.float32),
        ),
        in_specs=[VMEM] * 6,
        out_specs=(HBM, HBM),
        scratch_shapes=[
            pltpu.VMEM((peers, 8, 128), jnp.bfloat16),
            pltpu.VMEM(momentum.shape, jnp.float32),
            pltpu.SemaphoreType.DMA((PIECES + 1,)),
        ],
    )(squares.reshape(shards, 128), *assembled, momentum)
    update = update.reshape(2, peers // 2, 8, 128).transpose(0, 2, 1, 3).reshape(deltas.shape)
    return (update, new_momentum)


def solution(mesh):
    finer = Mesh(
        mesh.devices.reshape(4, 8, 2, mesh.shape["shard"]), ("path_0", "path_1", "path_2", "shard")
    )
    in_specs = (P(PATH, "shard", None), P(None, "shard", PATH), P())
    out_specs = (P(PATH, "shard", None), P(None, "shard", PATH))
    return jax.shard_map(local, mesh=finer, in_specs=in_specs, out_specs=out_specs, check_vma=False)
```

```python
import jax
import jax.numpy as jnp
from jax import lax
from jax.experimental import pallas as pl
from jax.experimental.pallas import tpu as pltpu
from jax.sharding import Mesh
from jax.sharding import PartitionSpec as P

PATH = ("path_0", "path_1", "path_2")
TILES = ("path_2", "path_0", "path_1")

outer_rate = 0.7
momentum_rate = 0.9
clip_ratio = 2.0

UPPER, SQUARES, CHUNK = 8, 9, 10
GRAD_BITS, LOWER_BITS = 19, 12
MOMENTUM_SCALE = 8191.0
SQUARES_SCALE = 128.0
FOLD = momentum_rate * momentum_rate / (1.0 + momentum_rate)
KERNEL_BYTES = 4 << 20
VMEM = pl.BlockSpec(memory_space=pltpu.VMEM)
SMEM = pl.BlockSpec(memory_space=pltpu.SMEM)
HBM = pl.BlockSpec(memory_space=pl.ANY)
PIECES = 4


def path_of(peer, chips):
    return (peer % chips) * 2 + peer // chips


def kernel(body, name, **kwargs):
    params = pltpu.CompilerParams(vmem_limit_bytes=KERNEL_BYTES)
    return pl.pallas_call(body, name=name, compiler_params=params, **kwargs)


def nearest(x):
    return jnp.floor(x + 0.5).astype(jnp.int32)


def momentum_kernel(
    module_ref, mine_ref, other_ref, chunk_ref, lower_ref, fold_ref, count_ref, upper, count
):
    peers, modules = chunk_ref.shape[0] // CHUNK, mine_ref.shape[0]
    for m in range(modules):
        count[m] = 0
    for q in range(peers):
        count[module_ref[q]] += 1
    first_core = lax.axis_index("path_2") == 0
    row = lax.broadcasted_iota(jnp.int32, (8, 128), 0)
    for m in range(modules):
        count_ref[m : m + 1, :] = jnp.full((1, 128), count[m].astype(jnp.float32))
        mine = jnp.where(first_core, mine_ref[m, 0:8, :], mine_ref[m, 8:16, :])
        other = jnp.where(first_core, other_ref[m, 0:8, :], other_ref[m, 8:16, :])
        momentum = jnp.concatenate(
            [jnp.where(first_core, mine, other), jnp.where(first_core, other, mine)], axis=1
        )
        whole = nearest(momentum * MOMENTUM_SCALE)
        fold_ref[m] = FOLD * (momentum - whole.astype(jnp.float32) * (1.0 / MOMENTUM_SCALE))
        whole += 32768
        lower_ref[m] = whole & ((1 << LOWER_BITS) - 1)
        word = (whole >> LOWER_BITS) << (row * 4)
        for rows in (4, 2, 1):
            word = word | pltpu.roll(word, rows, 0)
        upper[m] = word
    for q in range(peers):
        start = q * CHUNK
        m = module_ref[path_of(q, peers // 2)]
        chunk_ref[start + UPPER : start + SQUARES, :] = upper[m, 0:1, :]


def gather_kernel(
    module_ref, column_ref, lower_ref, fold_ref, count_ref, _, chunk_ref, chunk_out, grad_ref, *scratch
):
    *sums, words, sems = scratch
    peers, modules = column_ref.shape[0], grad_ref.shape[0]
    chips = peers // 2
    for total in sums:
        total[...] = jnp.zeros_like(total)
    for q in range(peers):
        m = module_ref[path_of(q, chips)]
        total = sums[q % len(sums)]
        total[m] += column_ref[q].astype(jnp.float32)
    for m in range(modules):
        total = sums[0][m]
        for more in sums[1:]:
            total += more[m]
        grad_ref[m] = total / count_ref[m : m + 1, :]
    grad = grad_ref[...]
    squares = jnp.sum(jnp.sum(grad * grad, axis=1), axis=1, keepdims=True)
    largest = jnp.max(jnp.max(jnp.abs(grad + fold_ref[...]), axis=1), axis=1, keepdims=True)
    power = jnp.ceil(jnp.log2(jnp.maximum(largest, 1e-30)))
    scale = jnp.exp2(GRAD_BITS - power)
    limit = 2.0**GRAD_BITS - 1.0
    for m in range(modules):
        exact = (grad_ref[m] + fold_ref[m]) * scale[m : m + 1, :]
        words[m] = (nearest(jnp.clip(exact, -limit, limit)) << LOWER_BITS) | lower_ref[m]
    row = lax.broadcasted_iota(jnp.int32, (modules, 128), 0)
    lane = lax.broadcasted_iota(jnp.int32, (modules, 128), 1)
    tail = jnp.where(row == lane, squares * SQUARES_SCALE, 0.0)
    tail = jnp.where(row + modules == lane, power, tail)
    tail = nearest(jnp.sum(tail, axis=0, keepdims=True))
    copies = []
    for q in range(peers):
        m = module_ref[path_of(q, chips)]
        start = q * CHUNK
        chunk_ref[start : start + UPPER, :] = words[m]
        chunk_ref[start + SQUARES : start + CHUNK, :] = tail
        if (q + 1) % (peers // PIECES) == 0:
            piece = pl.ds(len(copies) * (peers // PIECES) * CHUNK, (peers // PIECES) * CHUNK)
            sem = sems.at[len(copies)]
            copies.append(pltpu.make_async_copy(chunk_ref.at[piece], chunk_out.at[piece], sem))
            copies[-1].start()
    for copy in copies:
        copy.wait()


def assemble_kernel(
    module_ref, chunk_ref, mine_ref, other_ref, grad_ref, decay_ref, own_grad_ref, own_ref
):
    peers, modules = grad_ref.shape[0], mine_ref.shape[0]
    core = lax.axis_index("path_2")
    chip = lax.axis_index("path_0") * lax.axis_size("path_1") + lax.axis_index("path_1")
    module = module_ref[chip * 2 + core]
    tail = chunk_ref[pl.ds(SQUARES, peers, stride=CHUNK), :]
    lane = lax.broadcasted_iota(jnp.int32, (peers, 128), 1)
    power = jnp.where(lane == module + modules, tail, 0).astype(jnp.float32)
    power = jnp.sum(power, axis=1, keepdims=True)
    scale = jnp.broadcast_to(1.0 / jnp.exp2(GRAD_BITS - power), (peers, 128))
    row = lax.broadcasted_iota(jnp.int32, (8, 128), 0)
    for q in range(peers):
        start = q * CHUNK
        words = chunk_ref[start : start + UPPER, :]
        grad_ref[q] = (words >> LOWER_BITS).astype(jnp.float32) * scale[q : q + 1, :]
        upper = (chunk_ref[start + UPPER : start + SQUARES, :] >> (row * 4)) & 15
        whole = ((upper << LOWER_BITS) | (words & ((1 << LOWER_BITS) - 1))) - 32768
        decay_ref[q] = whole.astype(jnp.float32) * (momentum_rate / MOMENTUM_SCALE)
    for m in range(modules):
        for half in range(2):
            grad = jnp.where(core == half, mine_ref[m], other_ref[m])
            grad = jnp.where(core == 0, grad, pltpu.roll(grad, 64, 1))
            own_grad_ref[m, half * 8 : half * 8 + 8, :] = grad[:, 0:64]
    own_ref[...] = (lane[0:1, :] == module).astype(jnp.float32)


def step_kernel(
    limit, squares_ref, grad_ref, decay_ref, own_grad_ref, own_ref, momentum_ref,
    update_out, new_out, update, new, sems,
):
    peers, modules = update.shape[0], new.shape[0]
    norm_squares = jnp.sum(squares_ref[...], axis=0, keepdims=True)
    shrink = jnp.minimum(1.0, limit / jnp.sqrt(norm_squares + 1e-06))
    own = jnp.sum(jnp.where(own_ref[...] > 0.0, shrink, 0.0), axis=1, keepdims=True)
    each = peers // PIECES
    copies = []
    for piece in range(PIECES):
        tiles = slice(piece * each, (piece + 1) * each)
        clipped = grad_ref[tiles] * own.reshape(1, 1, 1)
        step = outer_rate * (clipped + momentum_rate * (decay_ref[tiles] + clipped))
        update[tiles] = step.astype(jnp.bfloat16)
        copies.append(pltpu.make_async_copy(update.at[tiles], update_out.at[tiles], sems.at[piece]))
        copies[-1].start()
    lane = lax.broadcasted_iota(jnp.int32, (1, 128), 1)
    for m in range(modules):
        k = jnp.sum(jnp.where(lane == m, shrink, 0.0), axis=1, keepdims=True)
        new[m] = momentum_rate * momentum_ref[m] + own_grad_ref[m] * k
    copies.append(pltpu.make_async_copy(new, new_out, sems.at[PIECES]))
    copies[-1].start()
    for copy in copies:
        copy.wait()


def local(deltas, momentum, path_module):
    modules, rows, width = momentum.shape
    columns = deltas.shape[2]
    peers = lax.axis_size(PATH)
    shards = lax.axis_size("shard")
    shape = jax.ShapeDtypeStruct
    tiles = deltas.reshape(2, 8, peers // 2, 128).transpose(0, 2, 1, 3).reshape(peers, 8, 128)
    column_tiles = lax.all_to_all(tiles, TILES, 0, 0, tiled=True)
    other = lax.ppermute(momentum, "path_2", [(0, 1), (1, 0)])
    module_tiles = shape((modules, 8, 128), jnp.float32)
    chunk_rows = shape((peers * CHUNK, 128), jnp.int32)
    chunks, *packed = kernel(
        momentum_kernel,
        "pack_momentum",
        out_shape=(
            chunk_rows,
            shape((modules, 8, 128), jnp.int32),
            module_tiles,
            shape((modules, 128), jnp.float32),
        ),
        in_specs=[SMEM, VMEM, VMEM],
        out_specs=(VMEM,) * 4,
        scratch_shapes=[
            pltpu.VMEM((modules, 8, 128), jnp.int32),
            pltpu.SMEM((modules,), jnp.int32),
        ],
    )(path_module, momentum, other)
    _, chunks, grad = kernel(
        gather_kernel,
        "gather_modules",
        out_shape=(chunk_rows, chunk_rows, module_tiles),
        in_specs=[SMEM, VMEM, VMEM, VMEM, VMEM, VMEM],
        out_specs=(VMEM, HBM, VMEM),
        input_output_aliases={5: 0},
        scratch_shapes=[pltpu.VMEM((modules, 8, 128), jnp.float32)] * 4
        + [
            pltpu.VMEM((modules, 8, 128), jnp.int32),
            pltpu.SemaphoreType.DMA((PIECES,)),
        ],
    )(path_module, column_tiles, *packed, chunks)
    chunks = lax.all_to_all(chunks.reshape(peers, CHUNK, 1, 128), TILES, 0, 0, tiled=True)
    other = lax.ppermute(grad, "path_2", [(0, 1), (1, 0)])
    chunks, other = lax.optimization_barrier((chunks, other))
    squares = jnp.sum(chunks[:, SQUARES].astype(jnp.float32) * (1.0 / SQUARES_SCALE), axis=0)
    squares = lax.all_to_all(
        jnp.broadcast_to(squares, (shards, 1, 128)), "shard", 0, 0, tiled=True
    )
    path_tiles = shape((peers, 8, 128), jnp.float32)
    assembled = kernel(
        assemble_kernel,
        "assemble",
        out_shape=(
            path_tiles,
            path_tiles,
            shape(momentum.shape, jnp.float32),
            shape((1, 128), jnp.float32),
        ),
        in_specs=[SMEM, VMEM, VMEM, VMEM],
        out_specs=(VMEM,) * 4,
    )(path_module, chunks.reshape(peers * CHUNK, 128), grad, other)
    limit = clip_ratio * float(rows * shards * columns) ** 0.5
    update, new_momentum = kernel(
        lambda *refs: step_kernel(limit, *refs),
        "step",
        out_shape=(
            shape((peers, 8, 128), jnp.bfloat16),
            shape(momentum.shape, jnp.float32),
        ),
        in_specs=[VMEM] * 6,
        out_specs=(HBM, HBM),
        scratch_shapes=[
            pltpu.VMEM((peers, 8, 128), jnp.bfloat16),
            pltpu.VMEM(momentum.shape, jnp.float32),
            pltpu.SemaphoreType.DMA((PIECES + 1,)),
        ],
    )(squares.reshape(shards, 128), *assembled, momentum)
    update = update.reshape(2, peers // 2, 8, 128).transpose(0, 2, 1, 3).reshape(deltas.shape)
    return (update, new_momentum)


def solution(mesh):
    finer = Mesh(
        mesh.devices.reshape(4, 8, 2, mesh.shape["shard"]), ("path_0", "path_1", "path_2", "shard")
    )
    in_specs = (P(PATH, "shard", None), P(None, "shard", PATH), P())
    out_specs = (P(PATH, "shard", None), P(None, "shard", PATH))
    return jax.shard_map(local, mesh=finer, in_specs=in_specs, out_specs=out_specs, check_vma=False)
```

```python
import jax
import jax.numpy as jnp
from jax import lax
from jax.experimental import pallas as pl
from jax.experimental.pallas import tpu as pltpu
from jax.sharding import Mesh
from jax.sharding import PartitionSpec as P

PATH = ("path_0", "path_1", "path_2")
TILES = ("path_2", "path_0", "path_1")

outer_rate = 0.7
momentum_rate = 0.9
clip_ratio = 2.0

UPPER, CHUNK = 8, 9
GRAD_BITS, LOWER_BITS = 18, 13
EXPONENTS, BIAS = 64, 128
MOMENTUM_SCALE = 8191.0
SQUARES_SCALE = 128.0
FOLD = momentum_rate * momentum_rate / (1.0 + momentum_rate)
KERNEL_BYTES = 4 << 20
VMEM = pl.BlockSpec(memory_space=pltpu.VMEM)
SMEM = pl.BlockSpec(memory_space=pltpu.SMEM)
HBM = pl.BlockSpec(memory_space=pl.ANY)
PIECES = 4


def path_of(peer, chips):
    return (peer % chips) * 2 + peer // chips


def kernel(body, name, **kwargs):
    params = pltpu.CompilerParams(vmem_limit_bytes=KERNEL_BYTES)
    return pl.pallas_call(body, name=name, compiler_params=params, **kwargs)


def lanes():
    return lax.broadcasted_iota(jnp.int32, (8, 128), 1)


def nearest(x):
    return jnp.floor(x + 0.5).astype(jnp.int32)


def momentum_kernel(
    module_ref, mine_ref, other_ref, lower_ref, upper_ref, fold_ref, count_ref, count
):
    peers, modules = module_ref.shape[0], mine_ref.shape[0]
    for m in range(modules):
        count[m] = 0
    for q in range(peers):
        count[module_ref[q]] += 1
    first_core = lax.axis_index("path_2") == 0
    row = lax.broadcasted_iota(jnp.int32, (8, 128), 0)
    for m in range(modules):
        count_ref[m : m + 1, :] = jnp.full((1, 128), count[m].astype(jnp.float32))
        mine = jnp.where(first_core, mine_ref[m, 0:8, :], mine_ref[m, 8:16, :])
        other = jnp.where(first_core, other_ref[m, 0:8, :], other_ref[m, 8:16, :])
        momentum = jnp.concatenate(
            [jnp.where(first_core, mine, other), jnp.where(first_core, other, mine)], axis=1
        )
        whole = nearest(momentum * MOMENTUM_SCALE)
        fold_ref[m] = FOLD * (momentum - whole.astype(jnp.float32) * (1.0 / MOMENTUM_SCALE))
        whole += 32768
        lower_ref[m] = whole & ((1 << LOWER_BITS) - 1)
        word = (whole >> LOWER_BITS) << (row * 3)
        for rows in (4, 2, 1):
            word = word | pltpu.roll(word, rows, 0)
        upper_ref[m : m + 1, :] = word[0:1, :]


def gather_kernel(
    module_ref, column_ref, lower_ref, upper_ref, fold_ref, count_ref, chunk_out, grad_ref, *scratch
):
    *sums, words, chunk, sems = scratch
    peers, modules = column_ref.shape[0], grad_ref.shape[0]
    chips = peers // 2
    for total in sums:
        total[...] = jnp.zeros_like(total)
    for q in range(peers):
        m = module_ref[path_of(q, chips)]
        total = sums[q % len(sums)]
        total[m] += column_ref[q].astype(jnp.float32)
    for m in range(modules):
        total = sums[0][m]
        for more in sums[1:]:
            total += more[m]
        grad_ref[m] = total / count_ref[m : m + 1, :]
    grad = grad_ref[...]
    squares = jnp.sum(jnp.sum(grad * grad, axis=1), axis=1, keepdims=True)
    squares = nearest(squares * SQUARES_SCALE)
    row = lax.broadcasted_iota(jnp.int32, (modules, 128), 0)
    lane = lax.broadcasted_iota(jnp.int32, (modules, 128), 1)
    norms = jnp.where(lane >> 2 == row, (squares >> ((lane & 3) * 8)) & 255, 0)
    norms = jnp.sum(norms.astype(jnp.float32), axis=0, keepdims=True)
    limit = 2.0**GRAD_BITS - 1.0
    own_lane = lanes() == EXPONENTS + lax.broadcasted_iota(jnp.int32, (8, 128), 0)
    for m in range(modules):
        exact = grad_ref[m] + fold_ref[m]
        largest = jnp.max(jnp.abs(exact), axis=1, keepdims=True)
        power = jnp.ceil(jnp.log2(jnp.maximum(largest, 1e-30)))
        exact = jnp.clip(exact * jnp.exp2(GRAD_BITS - power), -limit, limit)
        words[m, 0:UPPER, :] = (nearest(exact) << LOWER_BITS) | lower_ref[m]
        powers = jnp.sum(jnp.where(own_lane, power + BIAS, 0.0), axis=0, keepdims=True)
        words[m, UPPER:CHUNK, :] = upper_ref[m : m + 1, :] | ((norms + powers).astype(jnp.int32) << 24)
    copies = []
    for q in range(peers):
        m = module_ref[path_of(q, chips)]
        start = q * CHUNK
        chunk[start : start + UPPER, :] = words[m, 0:UPPER, :]
        chunk[start + UPPER : start + CHUNK, :] = words[m, UPPER:CHUNK, :]
        if (q + 1) % (peers // PIECES) == 0:
            piece = pl.ds(len(copies) * (peers // PIECES) * CHUNK, (peers // PIECES) * CHUNK)
            sem = sems.at[len(copies)]
            copies.append(pltpu.make_async_copy(chunk.at[piece], chunk_out.at[piece], sem))
            copies[-1].start()
    for copy in copies:
        copy.wait()


def assemble_kernel(
    module_ref, chunk_ref, mine_ref, other_ref, grad_ref, decay_ref, own_grad_ref, own_ref
):
    peers, modules = grad_ref.shape[0], mine_ref.shape[0]
    core = lax.axis_index("path_2")
    chip = lax.axis_index("path_0") * lax.axis_size("path_1") + lax.axis_index("path_1")
    module = module_ref[chip * 2 + core]
    power = (chunk_ref[pl.ds(UPPER, peers, stride=CHUNK), :] >> 24) & 255
    scale = 1.0 / jnp.exp2(GRAD_BITS + BIAS - power.astype(jnp.float32))
    row = lax.broadcasted_iota(jnp.int32, (8, 128), 0)
    own_lane = lanes() == EXPONENTS + row
    for q in range(peers):
        start = q * CHUNK
        words = chunk_ref[start : start + UPPER, :]
        of_row = jnp.sum(jnp.where(own_lane, scale[q : q + 1, :], 0.0), axis=1, keepdims=True)
        grad_ref[q] = (words >> LOWER_BITS).astype(jnp.float32) * of_row
        upper = (chunk_ref[start + UPPER : start + CHUNK, :] >> (row * 3)) & 7
        whole = ((upper << LOWER_BITS) | (words & ((1 << LOWER_BITS) - 1))) - 32768
        decay_ref[q] = whole.astype(jnp.float32) * (momentum_rate / MOMENTUM_SCALE)
    for m in range(modules):
        for half in range(2):
            grad = jnp.where(core == half, mine_ref[m], other_ref[m])
            grad = jnp.where(core == 0, grad, pltpu.roll(grad, 64, 1))
            own_grad_ref[m, half * 8 : half * 8 + 8, :] = grad[:, 0:64]
    own_ref[...] = (lanes()[0:1, :] == 4 * module).astype(jnp.float32)


def step_kernel(
    limit, squares_ref, grad_ref, decay_ref, own_grad_ref, own_ref, momentum_ref,
    update_out, new_out, update, new, sems,
):
    peers, modules = update.shape[0], new.shape[0]
    lane = lanes()
    norm_squares = jnp.broadcast_to(jnp.sum(squares_ref[...], axis=0, keepdims=True), (8, 128))
    for byte in range(4):
        weight = 256.0**byte / SQUARES_SCALE
        norm_squares = jnp.where(lane & 3 == byte, norm_squares * weight, norm_squares)
    norm_squares += pltpu.roll(norm_squares, 127, 1)
    norm_squares = (norm_squares + pltpu.roll(norm_squares, 126, 1))[0:1, :]
    shrink = jnp.minimum(1.0, limit / jnp.sqrt(norm_squares + 1e-06))
    own = jnp.sum(jnp.where(own_ref[...] > 0.0, shrink, 0.0), axis=1, keepdims=True)
    each = peers // PIECES
    copies = []
    for piece in range(PIECES):
        tiles = slice(piece * each, (piece + 1) * each)
        clipped = grad_ref[tiles] * own.reshape(1, 1, 1)
        step = outer_rate * (clipped + momentum_rate * (decay_ref[tiles] + clipped))
        update[tiles] = step.astype(jnp.bfloat16)
        copies.append(pltpu.make_async_copy(update.at[tiles], update_out.at[tiles], sems.at[piece]))
        copies[-1].start()
    for m in range(modules):
        k = jnp.sum(jnp.where(lane[0:1, :] == 4 * m, shrink, 0.0), axis=1, keepdims=True)
        new[m] = momentum_rate * momentum_ref[m] + own_grad_ref[m] * k
    copies.append(pltpu.make_async_copy(new, new_out, sems.at[PIECES]))
    copies[-1].start()
    for copy in copies:
        copy.wait()


def local(deltas, momentum, path_module):
    modules, rows, width = momentum.shape
    columns = deltas.shape[2]
    peers = lax.axis_size(PATH)
    shards = lax.axis_size("shard")
    shape = jax.ShapeDtypeStruct
    tiles = deltas.reshape(2, 8, peers // 2, 128).transpose(0, 2, 1, 3).reshape(peers, 8, 128)
    column_tiles = lax.all_to_all(tiles, TILES, 0, 0, tiled=True)
    other = lax.ppermute(momentum, "path_2", [(0, 1), (1, 0)])
    module_tiles = shape((modules, 8, 128), jnp.float32)
    packed = kernel(
        momentum_kernel,
        "pack_momentum",
        out_shape=(
            shape((modules, 8, 128), jnp.int32),
            shape((modules, 128), jnp.int32),
            module_tiles,
            shape((modules, 128), jnp.float32),
        ),
        in_specs=[SMEM, VMEM, VMEM],
        out_specs=(VMEM,) * 4,
        scratch_shapes=[pltpu.SMEM((modules,), jnp.int32)],
    )(path_module, momentum, other)
    chunks, grad = kernel(
        gather_kernel,
        "gather_modules",
        out_shape=(shape((peers * CHUNK, 128), jnp.int32), module_tiles),
        in_specs=[SMEM, VMEM, VMEM, VMEM, VMEM, VMEM],
        out_specs=(HBM, VMEM),
        scratch_shapes=[pltpu.VMEM((modules, 8, 128), jnp.float32)] * 4
        + [
            pltpu.VMEM((modules, 16, 128), jnp.int32),
            pltpu.VMEM((peers * CHUNK, 128), jnp.int32),
            pltpu.SemaphoreType.DMA((PIECES,)),
        ],
    )(path_module, column_tiles, *packed)
    chunks = lax.all_to_all(chunks.reshape(peers, CHUNK, 1, 128), TILES, 0, 0, tiled=True)
    other = lax.ppermute(grad, "path_2", [(0, 1), (1, 0)])
    chunks, other = lax.optimization_barrier((chunks, other))
    squares = lax.shift_right_logical(chunks[:, UPPER], 24).astype(jnp.float32)
    squares = jnp.sum(squares, axis=0)
    squares = lax.all_to_all(
        jnp.broadcast_to(squares, (shards, 1, 128)), "shard", 0, 0, tiled=True
    )
    path_tiles = shape((peers, 8, 128), jnp.float32)
    assembled = kernel(
        assemble_kernel,
        "assemble",
        out_shape=(
            path_tiles,
            path_tiles,
            shape(momentum.shape, jnp.float32),
            shape((1, 128), jnp.float32),
        ),
        in_specs=[SMEM, VMEM, VMEM, VMEM],
        out_specs=(VMEM,) * 4,
    )(path_module, chunks.reshape(peers * CHUNK, 128), grad, other)
    limit = clip_ratio * float(rows * shards * columns) ** 0.5
    update, new_momentum = kernel(
        lambda *refs: step_kernel(limit, *refs),
        "step",
        out_shape=(
            shape((peers, 8, 128), jnp.bfloat16),
            shape(momentum.shape, jnp.float32),
        ),
        in_specs=[VMEM] * 6,
        out_specs=(HBM, HBM),
        scratch_shapes=[
            pltpu.VMEM((peers, 8, 128), jnp.bfloat16),
            pltpu.VMEM(momentum.shape, jnp.float32),
            pltpu.SemaphoreType.DMA((PIECES + 1,)),
        ],
    )(squares.reshape(shards, 128), *assembled, momentum)
    update = update.reshape(2, peers // 2, 8, 128).transpose(0, 2, 1, 3).reshape(deltas.shape)
    return (update, new_momentum)


def solution(mesh):
    finer = Mesh(
        mesh.devices.reshape(4, 8, 2, mesh.shape["shard"]), ("path_0", "path_1", "path_2", "shard")
    )
    in_specs = (P(PATH, "shard", None), P(None, "shard", PATH), P())
    out_specs = (P(PATH, "shard", None), P(None, "shard", PATH))
    return jax.shard_map(local, mesh=finer, in_specs=in_specs, out_specs=out_specs, check_vma=False)
```

```python
import jax
import jax.numpy as jnp
from jax import lax
from jax.experimental import pallas as pl
from jax.experimental.pallas import tpu as pltpu
from jax.sharding import Mesh
from jax.sharding import PartitionSpec as P

PATH = ("path_0", "path_1", "path_2")
TILES = ("path_2", "path_0", "path_1")

outer_rate = 0.7
momentum_rate = 0.9
clip_ratio = 2.0

UPPER, CHUNK = 8, 9
GRAD_BITS, LOWER_BITS = 18, 13
EXPONENTS, BIAS = 64, 128
MOMENTUM_SCALE = 8191.0
SQUARES_SCALE = 128.0
FOLD = momentum_rate * momentum_rate / (1.0 + momentum_rate)
KERNEL_BYTES = 4 << 20
VMEM = pl.BlockSpec(memory_space=pltpu.VMEM)
SMEM = pl.BlockSpec(memory_space=pltpu.SMEM)
HBM = pl.BlockSpec(memory_space=pl.ANY)
PIECES = 4


def path_of(peer, chips):
    return (peer % chips) * 2 + peer // chips


def kernel(body, name, **kwargs):
    params = pltpu.CompilerParams(vmem_limit_bytes=KERNEL_BYTES)
    return pl.pallas_call(body, name=name, compiler_params=params, **kwargs)


def lanes():
    return lax.broadcasted_iota(jnp.int32, (8, 128), 1)


def nearest(x):
    return jnp.floor(x + 0.5).astype(jnp.int32)


def momentum_kernel(
    module_ref, mine_ref, other_ref, lower_ref, upper_ref, fold_ref, count_ref, own_ref, count
):
    peers, modules = module_ref.shape[0], mine_ref.shape[0]
    for m in range(modules):
        count[m] = 0
    for q in range(peers):
        count[module_ref[q]] += 1
    chip = lax.axis_index("path_0") * lax.axis_size("path_1") + lax.axis_index("path_1")
    module = module_ref[chip * 2 + lax.axis_index("path_2")]
    own_ref[...] = (lanes()[0:1, :] == 4 * module).astype(jnp.float32)
    first_core = lax.axis_index("path_2") == 0
    row = lax.broadcasted_iota(jnp.int32, (8, 128), 0)
    for m in range(modules):
        count_ref[m : m + 1, :] = jnp.full((1, 128), count[m].astype(jnp.float32))
        mine = jnp.where(first_core, mine_ref[m, 0:8, :], mine_ref[m, 8:16, :])
        other = jnp.where(first_core, other_ref[m, 0:8, :], other_ref[m, 8:16, :])
        momentum = jnp.concatenate(
            [jnp.where(first_core, mine, other), jnp.where(first_core, other, mine)], axis=1
        )
        whole = nearest(momentum * MOMENTUM_SCALE)
        fold_ref[m] = FOLD * (momentum - whole.astype(jnp.float32) * (1.0 / MOMENTUM_SCALE))
        whole += 32768
        lower_ref[m] = whole & ((1 << LOWER_BITS) - 1)
        word = (whole >> LOWER_BITS) << (row * 3)
        for rows in (4, 2, 1):
            word = word | pltpu.roll(word, rows, 0)
        upper_ref[m : m + 1, :] = word[0:1, :]


def gather_kernel(
    module_ref, column_ref, lower_ref, upper_ref, fold_ref, count_ref, chunk_out, grad_ref, *scratch
):
    *sums, words, chunk, sems = scratch
    peers, modules = column_ref.shape[0], grad_ref.shape[0]
    chips = peers // 2
    for total in sums:
        total[...] = jnp.zeros_like(total)
    for q in range(peers):
        m = module_ref[path_of(q, chips)]
        total = sums[q % len(sums)]
        total[m] += column_ref[q].astype(jnp.float32)
    for m in range(modules):
        total = sums[0][m]
        for more in sums[1:]:
            total += more[m]
        grad_ref[m] = total / count_ref[m : m + 1, :]
    grad = grad_ref[...]
    squares = jnp.sum(jnp.sum(grad * grad, axis=1), axis=1, keepdims=True)
    squares = nearest(squares * SQUARES_SCALE)
    row = lax.broadcasted_iota(jnp.int32, (modules, 128), 0)
    lane = lax.broadcasted_iota(jnp.int32, (modules, 128), 1)
    norms = jnp.where(lane >> 2 == row, (squares >> ((lane & 3) * 8)) & 255, 0)
    norms = jnp.sum(norms.astype(jnp.float32), axis=0, keepdims=True)
    limit = 2.0**GRAD_BITS - 1.0
    own_lane = lanes() == EXPONENTS + lax.broadcasted_iota(jnp.int32, (8, 128), 0)
    for m in range(modules):
        exact = grad_ref[m] + fold_ref[m]
        largest = jnp.max(jnp.abs(exact), axis=1, keepdims=True)
        power = jnp.ceil(jnp.log2(jnp.maximum(largest, 1e-30)))
        exact = jnp.clip(exact * jnp.exp2(GRAD_BITS - power), -limit, limit)
        words[m, 0:UPPER, :] = (nearest(exact) << LOWER_BITS) | lower_ref[m]
        powers = jnp.sum(jnp.where(own_lane, power + BIAS, 0.0), axis=0, keepdims=True)
        words[m, UPPER:CHUNK, :] = upper_ref[m : m + 1, :] | ((norms + powers).astype(jnp.int32) << 24)
    copies = []
    for q in range(peers):
        m = module_ref[path_of(q, chips)]
        start = q * CHUNK
        chunk[start : start + UPPER, :] = words[m, 0:UPPER, :]
        chunk[start + UPPER : start + CHUNK, :] = words[m, UPPER:CHUNK, :]
        if (q + 1) % (peers // PIECES) == 0:
            piece = pl.ds(len(copies) * (peers // PIECES) * CHUNK, (peers // PIECES) * CHUNK)
            sem = sems.at[len(copies)]
            copies.append(pltpu.make_async_copy(chunk.at[piece], chunk_out.at[piece], sem))
            copies[-1].start()
    for copy in copies:
        copy.wait()


def columns_kernel(mine_ref, other_ref, grad_ref):
    core = lax.axis_index("path_2")
    for m in range(mine_ref.shape[0]):
        for half in range(2):
            grad = jnp.where(core == half, mine_ref[m], other_ref[m])
            grad = jnp.where(core == 0, grad, pltpu.roll(grad, 64, 1))
            grad_ref[m, half * 8 : half * 8 + 8, :] = grad[:, 0:64]


def step_kernel(
    limit, squares_ref, chunk_ref, own_grad_ref, own_ref, momentum_ref,
    update_out, new_out, update, new, sems,
):
    peers, modules = update.shape[0], new.shape[0]
    lane = lanes()
    norm_squares = jnp.broadcast_to(jnp.sum(squares_ref[...], axis=0, keepdims=True), (8, 128))
    for byte in range(4):
        weight = 256.0**byte / SQUARES_SCALE
        norm_squares = jnp.where(lane & 3 == byte, norm_squares * weight, norm_squares)
    norm_squares += pltpu.roll(norm_squares, 127, 1)
    norm_squares = (norm_squares + pltpu.roll(norm_squares, 126, 1))[0:1, :]
    shrink = jnp.minimum(1.0, limit / jnp.sqrt(norm_squares + 1e-06))
    own = jnp.sum(jnp.where(own_ref[...] > 0.0, shrink, 0.0), axis=1, keepdims=True)
    power = lax.shift_right_logical(chunk_ref[pl.ds(UPPER, peers, stride=CHUNK), :], 24)
    scale = own / jnp.exp2(GRAD_BITS + BIAS - power.astype(jnp.float32))
    row = lax.broadcasted_iota(jnp.int32, (8, 128), 0)
    own_lane = lane == EXPONENTS + row
    each = peers // PIECES
    copies = []
    for q in range(peers):
        start = q * CHUNK
        words = chunk_ref[start : start + UPPER, :]
        of_row = jnp.sum(jnp.where(own_lane, scale[q : q + 1, :], 0.0), axis=1, keepdims=True)
        clipped = (words >> LOWER_BITS).astype(jnp.float32) * of_row
        upper = (chunk_ref[start + UPPER : start + CHUNK, :] >> (row * 3)) & 7
        whole = ((upper << LOWER_BITS) | (words & ((1 << LOWER_BITS) - 1))) - 32768
        decay = whole.astype(jnp.float32) * (momentum_rate / MOMENTUM_SCALE)
        step = outer_rate * (clipped + momentum_rate * (decay + clipped))
        update[q] = step.astype(jnp.bfloat16)
        if (q + 1) % each == 0:
            piece = pl.ds(q + 1 - each, each)
            sem = sems.at[len(copies)]
            copies.append(pltpu.make_async_copy(update.at[piece], update_out.at[piece], sem))
            copies[-1].start()
    for m in range(modules):
        k = jnp.sum(jnp.where(lane[0:1, :] == 4 * m, shrink, 0.0), axis=1, keepdims=True)
        new[m] = momentum_rate * momentum_ref[m] + own_grad_ref[m] * k
    copies.append(pltpu.make_async_copy(new, new_out, sems.at[PIECES]))
    copies[-1].start()
    for copy in copies:
        copy.wait()


def local(deltas, momentum, path_module):
    modules, rows, width = momentum.shape
    columns = deltas.shape[2]
    peers = lax.axis_size(PATH)
    shards = lax.axis_size("shard")
    shape = jax.ShapeDtypeStruct
    tiles = deltas.reshape(2, 8, peers // 2, 128).transpose(0, 2, 1, 3).reshape(peers, 8, 128)
    column_tiles = lax.all_to_all(tiles, TILES, 0, 0, tiled=True)
    other = lax.ppermute(momentum, "path_2", [(0, 1), (1, 0)])
    module_tiles = shape((modules, 8, 128), jnp.float32)
    *packed, own = kernel(
        momentum_kernel,
        "pack_momentum",
        out_shape=(
            shape((modules, 8, 128), jnp.int32),
            shape((modules, 128), jnp.int32),
            module_tiles,
            shape((modules, 128), jnp.float32),
            shape((1, 128), jnp.float32),
        ),
        in_specs=[SMEM, VMEM, VMEM],
        out_specs=(VMEM,) * 5,
        scratch_shapes=[pltpu.SMEM((modules,), jnp.int32)],
    )(path_module, momentum, other)
    chunks, grad = kernel(
        gather_kernel,
        "gather_modules",
        out_shape=(shape((peers * CHUNK, 128), jnp.int32), module_tiles),
        in_specs=[SMEM, VMEM, VMEM, VMEM, VMEM, VMEM],
        out_specs=(HBM, VMEM),
        scratch_shapes=[pltpu.VMEM((modules, 8, 128), jnp.float32)] * 4
        + [
            pltpu.VMEM((modules, 16, 128), jnp.int32),
            pltpu.VMEM((peers * CHUNK, 128), jnp.int32),
            pltpu.SemaphoreType.DMA((PIECES,)),
        ],
    )(path_module, column_tiles, *packed)
    chunks = lax.all_to_all(chunks.reshape(peers, CHUNK, 1, 128), TILES, 0, 0, tiled=True)
    other = lax.ppermute(grad, "path_2", [(0, 1), (1, 0)])
    columns_grad = kernel(
        columns_kernel,
        "state_columns",
        out_shape=shape(momentum.shape, jnp.float32),
        in_specs=[VMEM] * 2,
        out_specs=VMEM,
    )(grad, other)
    chunks, columns_grad = lax.optimization_barrier((chunks, columns_grad))
    squares = lax.shift_right_logical(chunks[:, UPPER], 24).astype(jnp.float32)
    squares = jnp.sum(squares, axis=0)
    squares = lax.all_to_all(
        jnp.broadcast_to(squares, (shards, 1, 128)), "shard", 0, 0, tiled=True
    )
    limit = clip_ratio * float(rows * shards * columns) ** 0.5
    update, new_momentum = kernel(
        lambda *refs: step_kernel(limit, *refs),
        "step",
        out_shape=(
            shape((peers, 8, 128), jnp.bfloat16),
            shape(momentum.shape, jnp.float32),
        ),
        in_specs=[VMEM] * 5,
        out_specs=(HBM, HBM),
        scratch_shapes=[
            pltpu.VMEM((peers, 8, 128), jnp.bfloat16),
            pltpu.VMEM(momentum.shape, jnp.float32),
            pltpu.SemaphoreType.DMA((PIECES + 1,)),
        ],
    )(
        squares.reshape(shards, 128),
        chunks.reshape(peers * CHUNK, 128),
        columns_grad,
        own,
        momentum,
    )
    update = update.reshape(2, peers // 2, 8, 128).transpose(0, 2, 1, 3).reshape(deltas.shape)
    return (update, new_momentum)


def solution(mesh):
    finer = Mesh(
        mesh.devices.reshape(4, 8, 2, mesh.shape["shard"]), ("path_0", "path_1", "path_2", "shard")
    )
    in_specs = (P(PATH, "shard", None), P(None, "shard", PATH), P())
    out_specs = (P(PATH, "shard", None), P(None, "shard", PATH))
    return jax.shard_map(local, mesh=finer, in_specs=in_specs, out_specs=out_specs, check_vma=False)
```

```python
import jax
import jax.numpy as jnp
from jax import lax
from jax.experimental import pallas as pl
from jax.experimental.pallas import tpu as pltpu
from jax.sharding import Mesh
from jax.sharding import PartitionSpec as P

PATH = ("path_0", "path_1", "path_2")
TILES = ("path_2", "path_0", "path_1")

outer_rate = 0.7
momentum_rate = 0.9
clip_ratio = 2.0

UPPER, CHUNK = 8, 9
GRAD_BITS, LOWER_BITS = 18, 13
EXPONENTS, BIAS = 64, 128
MODULE_BITS, PACKED = 4, 8
MOMENTUM_SCALE = 8191.0
SQUARES_SCALE = 128.0
FOLD = momentum_rate * momentum_rate / (1.0 + momentum_rate)
KERNEL_BYTES = 4 << 20
VMEM = pl.BlockSpec(memory_space=pltpu.VMEM)
SMEM = pl.BlockSpec(memory_space=pltpu.SMEM)
HBM = pl.BlockSpec(memory_space=pl.ANY)
PIECES = 4


def path_of(peer, chips):
    return (peer % chips) * 2 + peer // chips


def kernel(body, name, **kwargs):
    params = pltpu.CompilerParams(vmem_limit_bytes=KERNEL_BYTES)
    return pl.pallas_call(body, name=name, compiler_params=params, **kwargs)


def lanes():
    return lax.broadcasted_iota(jnp.int32, (8, 128), 1)


def nearest(x):
    return jnp.floor(x + 0.5).astype(jnp.int32)


def momentum_kernel(
    module_ref, mine_ref, other_ref,
    lower_ref, upper_ref, fold_ref, count_ref, peer_ref, own_ref, count,
):
    peers, modules = module_ref.shape[0], mine_ref.shape[0]
    for m in range(modules):
        count[m] = 0
    for q in range(peers):
        count[module_ref[q]] += 1
    for word in range(peers // PACKED):
        packed = 0
        for k in range(PACKED):
            m = module_ref[path_of(word * PACKED + k, peers // 2)]
            packed = packed | (m << (k * MODULE_BITS))
        peer_ref[word : word + 1, :] = jnp.full((1, 128), packed)
    chip = lax.axis_index("path_0") * lax.axis_size("path_1") + lax.axis_index("path_1")
    module = module_ref[chip * 2 + lax.axis_index("path_2")]
    own_ref[...] = (lanes()[0:1, :] == 4 * module).astype(jnp.float32)
    first_core = lax.axis_index("path_2") == 0
    row = lax.broadcasted_iota(jnp.int32, (8, 128), 0)
    for m in range(modules):
        count_ref[m : m + 1, :] = jnp.full((1, 128), count[m].astype(jnp.float32))
        mine = jnp.where(first_core, mine_ref[m, 0:8, :], mine_ref[m, 8:16, :])
        other = jnp.where(first_core, other_ref[m, 0:8, :], other_ref[m, 8:16, :])
        momentum = jnp.concatenate(
            [jnp.where(first_core, mine, other), jnp.where(first_core, other, mine)], axis=1
        )
        whole = nearest(momentum * MOMENTUM_SCALE)
        fold_ref[m] = FOLD * (momentum - whole.astype(jnp.float32) * (1.0 / MOMENTUM_SCALE))
        whole += 32768
        lower_ref[m] = whole & ((1 << LOWER_BITS) - 1)
        word = (whole >> LOWER_BITS) << (row * 3)
        for rows in (4, 2, 1):
            word = word | pltpu.roll(word, rows, 0)
        upper_ref[m : m + 1, :] = word[0:1, :]


def gather_kernel(
    column_ref, lower_ref, upper_ref, fold_ref, count_ref, peer_ref, chunk_out, grad_ref, *scratch
):
    *sums, words, chunk, sems = scratch
    peers, modules = column_ref.shape[0], grad_ref.shape[0]
    packed = [peer_ref[word, 0] for word in range(peers // PACKED)]
    module_of = [
        (packed[q // PACKED] >> (q % PACKED * MODULE_BITS)) & (2**MODULE_BITS - 1)
        for q in range(peers)
    ]
    for total in sums:
        total[...] = jnp.zeros_like(total)
    for q in range(peers):
        m = module_of[q]
        total = sums[q % len(sums)]
        total[m] += column_ref[q].astype(jnp.float32)
    for m in range(modules):
        total = sums[0][m]
        for more in sums[1:]:
            total += more[m]
        grad_ref[m] = total / count_ref[m : m + 1, :]
    grad = grad_ref[...]
    squares = jnp.sum(jnp.sum(grad * grad, axis=1), axis=1, keepdims=True)
    squares = nearest(squares * SQUARES_SCALE)
    row = lax.broadcasted_iota(jnp.int32, (modules, 128), 0)
    lane = lax.broadcasted_iota(jnp.int32, (modules, 128), 1)
    norms = jnp.where(lane >> 2 == row, (squares >> ((lane & 3) * 8)) & 255, 0)
    norms = jnp.sum(norms.astype(jnp.float32), axis=0, keepdims=True)
    limit = 2.0**GRAD_BITS - 1.0
    own_lane = lanes() == EXPONENTS + lax.broadcasted_iota(jnp.int32, (8, 128), 0)
    for m in range(modules):
        exact = grad_ref[m] + fold_ref[m]
        largest = jnp.max(jnp.abs(exact), axis=1, keepdims=True)
        power = jnp.ceil(jnp.log2(jnp.maximum(largest, 1e-30)))
        exact = jnp.clip(exact * jnp.exp2(GRAD_BITS - power), -limit, limit)
        words[m, 0:UPPER, :] = (nearest(exact) << LOWER_BITS) | lower_ref[m]
        powers = jnp.sum(jnp.where(own_lane, power + BIAS, 0.0), axis=0, keepdims=True)
        words[m, UPPER:CHUNK, :] = upper_ref[m : m + 1, :] | ((norms + powers).astype(jnp.int32) << 24)
    copies = []
    for q in range(peers):
        m = module_of[q]
        start = q * CHUNK
        chunk[start : start + UPPER, :] = words[m, 0:UPPER, :]
        chunk[start + UPPER : start + CHUNK, :] = words[m, UPPER:CHUNK, :]
        if (q + 1) % (peers // PIECES) == 0:
            piece = pl.ds(len(copies) * (peers // PIECES) * CHUNK, (peers // PIECES) * CHUNK)
            sem = sems.at[len(copies)]
            copies.append(pltpu.make_async_copy(chunk.at[piece], chunk_out.at[piece], sem))
            copies[-1].start()
    for copy in copies:
        copy.wait()


def columns_kernel(mine_ref, other_ref, grad_ref):
    core = lax.axis_index("path_2")
    for m in range(mine_ref.shape[0]):
        for half in range(2):
            grad = jnp.where(core == half, mine_ref[m], other_ref[m])
            grad = jnp.where(core == 0, grad, pltpu.roll(grad, 64, 1))
            grad_ref[m, half * 8 : half * 8 + 8, :] = grad[:, 0:64]


def step_kernel(
    limit, squares_ref, chunk_ref, own_grad_ref, own_ref, momentum_ref,
    update_out, new_out, update, new, sems,
):
    peers, modules = update.shape[0], new.shape[0]
    lane = lanes()
    norm_squares = jnp.broadcast_to(jnp.sum(squares_ref[...], axis=0, keepdims=True), (8, 128))
    for byte in range(4):
        weight = 256.0**byte / SQUARES_SCALE
        norm_squares = jnp.where(lane & 3 == byte, norm_squares * weight, norm_squares)
    norm_squares += pltpu.roll(norm_squares, 127, 1)
    norm_squares = (norm_squares + pltpu.roll(norm_squares, 126, 1))[0:1, :]
    shrink = jnp.minimum(1.0, limit / jnp.sqrt(norm_squares + 1e-06))
    own = jnp.sum(jnp.where(own_ref[...] > 0.0, shrink, 0.0), axis=1, keepdims=True)
    power = lax.shift_right_logical(chunk_ref[pl.ds(UPPER, peers, stride=CHUNK), :], 24)
    scale = own / jnp.exp2(GRAD_BITS + BIAS - power.astype(jnp.float32))
    row = lax.broadcasted_iota(jnp.int32, (8, 128), 0)
    own_lane = lane == EXPONENTS + row
    each = peers // PIECES
    copies = []
    for q in range(peers):
        start = q * CHUNK
        words = chunk_ref[start : start + UPPER, :]
        of_row = jnp.sum(jnp.where(own_lane, scale[q : q + 1, :], 0.0), axis=1, keepdims=True)
        clipped = (words >> LOWER_BITS).astype(jnp.float32) * of_row
        upper = (chunk_ref[start + UPPER : start + CHUNK, :] >> (row * 3)) & 7
        whole = ((upper << LOWER_BITS) | (words & ((1 << LOWER_BITS) - 1))) - 32768
        decay = whole.astype(jnp.float32) * (momentum_rate / MOMENTUM_SCALE)
        step = outer_rate * (clipped + momentum_rate * (decay + clipped))
        update[q] = step.astype(jnp.bfloat16)
        if (q + 1) % each == 0:
            piece = pl.ds(q + 1 - each, each)
            sem = sems.at[len(copies)]
            copies.append(pltpu.make_async_copy(update.at[piece], update_out.at[piece], sem))
            copies[-1].start()
    for m in range(modules):
        k = jnp.sum(jnp.where(lane[0:1, :] == 4 * m, shrink, 0.0), axis=1, keepdims=True)
        new[m] = momentum_rate * momentum_ref[m] + own_grad_ref[m] * k
    copies.append(pltpu.make_async_copy(new, new_out, sems.at[PIECES]))
    copies[-1].start()
    for copy in copies:
        copy.wait()


def local(deltas, momentum, path_module):
    modules, rows, width = momentum.shape
    columns = deltas.shape[2]
    peers = lax.axis_size(PATH)
    shards = lax.axis_size("shard")
    shape = jax.ShapeDtypeStruct
    tiles = deltas.reshape(2, 8, peers // 2, 128).transpose(0, 2, 1, 3).reshape(peers, 8, 128)
    column_tiles = lax.all_to_all(tiles, TILES, 0, 0, tiled=True)
    other = lax.ppermute(momentum, "path_2", [(0, 1), (1, 0)])
    module_tiles = shape((modules, 8, 128), jnp.float32)
    *packed, own = kernel(
        momentum_kernel,
        "pack_momentum",
        out_shape=(
            shape((modules, 8, 128), jnp.int32),
            shape((modules, 128), jnp.int32),
            module_tiles,
            shape((modules, 128), jnp.float32),
            shape((peers // PACKED, 128), jnp.int32),
            shape((1, 128), jnp.float32),
        ),
        in_specs=[SMEM, VMEM, VMEM],
        out_specs=(VMEM,) * 6,
        scratch_shapes=[pltpu.SMEM((modules,), jnp.int32)],
    )(path_module, momentum, other)
    chunks, grad = kernel(
        gather_kernel,
        "gather_modules",
        out_shape=(shape((peers * CHUNK, 128), jnp.int32), module_tiles),
        in_specs=[VMEM] * 6,
        out_specs=(HBM, VMEM),
        scratch_shapes=[pltpu.VMEM((modules, 8, 128), jnp.float32)] * 4
        + [
            pltpu.VMEM((modules, 16, 128), jnp.int32),
            pltpu.VMEM((peers * CHUNK, 128), jnp.int32),
            pltpu.SemaphoreType.DMA((PIECES,)),
        ],
    )(column_tiles, *packed)
    chunks = lax.all_to_all(chunks.reshape(peers, CHUNK, 1, 128), TILES, 0, 0, tiled=True)
    other = lax.ppermute(grad, "path_2", [(0, 1), (1, 0)])
    columns_grad = kernel(
        columns_kernel,
        "state_columns",
        out_shape=shape(momentum.shape, jnp.float32),
        in_specs=[VMEM] * 2,
        out_specs=VMEM,
    )(grad, other)
    chunks, columns_grad = lax.optimization_barrier((chunks, columns_grad))
    squares = lax.shift_right_logical(chunks[:, UPPER], 24).astype(jnp.float32)
    squares = jnp.sum(squares, axis=0)
    squares = lax.all_to_all(
        jnp.broadcast_to(squares, (shards, 1, 128)), "shard", 0, 0, tiled=True
    )
    limit = clip_ratio * float(rows * shards * columns) ** 0.5
    update, new_momentum = kernel(
        lambda *refs: step_kernel(limit, *refs),
        "step",
        out_shape=(
            shape((peers, 8, 128), jnp.bfloat16),
            shape(momentum.shape, jnp.float32),
        ),
        in_specs=[VMEM] * 5,
        out_specs=(HBM, HBM),
        scratch_shapes=[
            pltpu.VMEM((peers, 8, 128), jnp.bfloat16),
            pltpu.VMEM(momentum.shape, jnp.float32),
            pltpu.SemaphoreType.DMA((PIECES + 1,)),
        ],
    )(
        squares.reshape(shards, 128),
        chunks.reshape(peers * CHUNK, 128),
        columns_grad,
        own,
        momentum,
    )
    update = update.reshape(2, peers // 2, 8, 128).transpose(0, 2, 1, 3).reshape(deltas.shape)
    return (update, new_momentum)


def solution(mesh):
    finer = Mesh(
        mesh.devices.reshape(4, 8, 2, mesh.shape["shard"]), ("path_0", "path_1", "path_2", "shard")
    )
    in_specs = (P(PATH, "shard", None), P(None, "shard", PATH), P())
    out_specs = (P(PATH, "shard", None), P(None, "shard", PATH))
    return jax.shard_map(local, mesh=finer, in_specs=in_specs, out_specs=out_specs, check_vma=False)
```

```python
import jax
import jax.numpy as jnp
from jax import lax
from jax.experimental import pallas as pl
from jax.experimental.pallas import tpu as pltpu
from jax.sharding import Mesh
from jax.sharding import PartitionSpec as P

PATH = ("path_0", "path_1", "path_2")
TILES = ("path_2", "path_0", "path_1")

outer_rate = 0.7
momentum_rate = 0.9
clip_ratio = 2.0

UPPER, CHUNK = 8, 9
GRAD_BITS, LOWER_BITS = 18, 13
EXPONENTS, BIAS = 64, 128
MODULE_BITS, PACKED = 4, 8
MOMENTUM_SCALE = 8191.0
SQUARES_SCALE = 128.0
FOLD = momentum_rate * momentum_rate / (1.0 + momentum_rate)
KERNEL_BYTES = 4 << 20
VMEM = pl.BlockSpec(memory_space=pltpu.VMEM)
SMEM = pl.BlockSpec(memory_space=pltpu.SMEM)
HBM = pl.BlockSpec(memory_space=pl.ANY)
PIECES = 4


def path_of(peer, chips):
    return (peer % chips) * 2 + peer // chips


def kernel(body, name, **kwargs):
    params = pltpu.CompilerParams(vmem_limit_bytes=KERNEL_BYTES)
    return pl.pallas_call(body, name=name, compiler_params=params, **kwargs)


def lanes():
    return lax.broadcasted_iota(jnp.int32, (8, 128), 1)


def nearest(x):
    return jnp.floor(x + 0.5).astype(jnp.int32)


def momentum_kernel(
    module_ref, mine_ref, other_ref,
    lower_ref, upper_ref, fold_ref, count_ref, peer_ref, own_ref, count,
):
    peers, modules = module_ref.shape[0], mine_ref.shape[0]
    for m in range(modules):
        count[m] = 0
    for q in range(peers):
        count[module_ref[q]] += 1
    for word in range(peers // PACKED):
        packed = 0
        for k in range(PACKED):
            m = module_ref[path_of(word * PACKED + k, peers // 2)]
            packed = packed | (m << (k * MODULE_BITS))
        peer_ref[word : word + 1, :] = jnp.full((1, 128), packed)
    chip = lax.axis_index("path_0") * lax.axis_size("path_1") + lax.axis_index("path_1")
    module = module_ref[chip * 2 + lax.axis_index("path_2")]
    own_ref[...] = (lanes()[0:1, :] == 4 * module).astype(jnp.float32)
    first_core = lax.axis_index("path_2") == 0
    row = lax.broadcasted_iota(jnp.int32, (8, 128), 0)
    for m in range(modules):
        count_ref[m : m + 1, :] = jnp.full((1, 128), count[m].astype(jnp.float32))
        mine = jnp.where(first_core, mine_ref[m, 0:8, :], mine_ref[m, 8:16, :])
        other = jnp.where(first_core, other_ref[m, 0:8, :], other_ref[m, 8:16, :])
        momentum = jnp.concatenate(
            [jnp.where(first_core, mine, other), jnp.where(first_core, other, mine)], axis=1
        )
        whole = nearest(momentum * MOMENTUM_SCALE)
        fold_ref[m] = FOLD * (momentum - whole.astype(jnp.float32) * (1.0 / MOMENTUM_SCALE))
        whole += 32768
        lower_ref[m] = whole & ((1 << LOWER_BITS) - 1)
        word = (whole >> LOWER_BITS) << (row * 3)
        for rows in (4, 2, 1):
            word = word | pltpu.roll(word, rows, 0)
        upper_ref[m : m + 1, :] = word[0:1, :]


def gather_kernel(
    column_ref, lower_ref, upper_ref, fold_ref, count_ref, peer_ref, chunk_ref, grad_ref, *scratch
):
    *sums, words = scratch
    peers, modules = column_ref.shape[0], grad_ref.shape[0]
    packed = [peer_ref[word, 0] for word in range(peers // PACKED)]
    module_of = [
        (packed[q // PACKED] >> (q % PACKED * MODULE_BITS)) & (2**MODULE_BITS - 1)
        for q in range(peers)
    ]
    for total in sums:
        total[...] = jnp.zeros_like(total)
    for q in range(peers):
        m = module_of[q]
        total = sums[q % len(sums)]
        total[m] += column_ref[q].astype(jnp.float32)
    for m in range(modules):
        total = sums[0][m]
        for more in sums[1:]:
            total += more[m]
        grad_ref[m] = total / count_ref[m : m + 1, :]
    grad = grad_ref[...]
    squares = jnp.sum(jnp.sum(grad * grad, axis=1), axis=1, keepdims=True)
    squares = nearest(squares * SQUARES_SCALE)
    row = lax.broadcasted_iota(jnp.int32, (modules, 128), 0)
    lane = lax.broadcasted_iota(jnp.int32, (modules, 128), 1)
    norms = jnp.where(lane >> 2 == row, (squares >> ((lane & 3) * 8)) & 255, 0)
    norms = jnp.sum(norms.astype(jnp.float32), axis=0, keepdims=True)
    limit = 2.0**GRAD_BITS - 1.0
    own_lane = lanes() == EXPONENTS + lax.broadcasted_iota(jnp.int32, (8, 128), 0)
    for m in range(modules):
        exact = grad_ref[m] + fold_ref[m]
        largest = jnp.max(jnp.abs(exact), axis=1, keepdims=True)
        power = jnp.ceil(jnp.log2(jnp.maximum(largest, 1e-30)))
        exact = jnp.clip(exact * jnp.exp2(GRAD_BITS - power), -limit, limit)
        words[m, 0:UPPER, :] = (nearest(exact) << LOWER_BITS) | lower_ref[m]
        powers = jnp.sum(jnp.where(own_lane, power + BIAS, 0.0), axis=0, keepdims=True)
        words[m, UPPER:CHUNK, :] = upper_ref[m : m + 1, :] | ((norms + powers).astype(jnp.int32) << 24)
    for q in range(peers):
        m = module_of[q]
        start = q * CHUNK
        chunk_ref[start : start + UPPER, :] = words[m, 0:UPPER, :]
        chunk_ref[start + UPPER : start + CHUNK, :] = words[m, UPPER:CHUNK, :]


def assemble_kernel(chunk_ref, own_ref, grad_ref, decay_ref, mask_ref):
    peers = grad_ref.shape[0]
    power = lax.shift_right_logical(chunk_ref[pl.ds(UPPER, peers, stride=CHUNK), :], 24)
    scale = 1.0 / jnp.exp2(GRAD_BITS + BIAS - power.astype(jnp.float32))
    row = lax.broadcasted_iota(jnp.int32, (8, 128), 0)
    own_lane = lanes() == EXPONENTS + row
    for q in range(peers):
        start = q * CHUNK
        words = chunk_ref[start : start + UPPER, :]
        of_row = jnp.sum(jnp.where(own_lane, scale[q : q + 1, :], 0.0), axis=1, keepdims=True)
        grad_ref[q] = (words >> LOWER_BITS).astype(jnp.float32) * of_row
        upper = (chunk_ref[start + UPPER : start + CHUNK, :] >> (row * 3)) & 7
        whole = ((upper << LOWER_BITS) | (words & ((1 << LOWER_BITS) - 1))) - 32768
        decay_ref[q] = whole.astype(jnp.float32) * (momentum_rate / MOMENTUM_SCALE)
    mask_ref[...] = own_ref[...]


def columns_kernel(mine_ref, other_ref, mask_ref, grad_ref, own_ref):
    core = lax.axis_index("path_2")
    for m in range(mine_ref.shape[0]):
        for half in range(2):
            grad = jnp.where(core == half, mine_ref[m], other_ref[m])
            grad = jnp.where(core == 0, grad, pltpu.roll(grad, 64, 1))
            grad_ref[m, half * 8 : half * 8 + 8, :] = grad[:, 0:64]
    own_ref[...] = mask_ref[...]


def step_kernel(
    limit, squares_ref, grad_ref, decay_ref, own_grad_ref, own_ref, momentum_ref,
    update_out, new_out, update, new, sems,
):
    peers, modules = update.shape[0], new.shape[0]
    lane = lanes()
    norm_squares = jnp.broadcast_to(jnp.sum(squares_ref[...], axis=0, keepdims=True), (8, 128))
    for byte in range(4):
        weight = 256.0**byte / SQUARES_SCALE
        norm_squares = jnp.where(lane & 3 == byte, norm_squares * weight, norm_squares)
    norm_squares += pltpu.roll(norm_squares, 127, 1)
    norm_squares = (norm_squares + pltpu.roll(norm_squares, 126, 1))[0:1, :]
    shrink = jnp.minimum(1.0, limit / jnp.sqrt(norm_squares + 1e-06))
    own = jnp.sum(jnp.where(own_ref[...] > 0.0, shrink, 0.0), axis=1, keepdims=True)
    each = peers // PIECES
    copies = []
    for piece in range(PIECES):
        tiles = slice(piece * each, (piece + 1) * each)
        clipped = grad_ref[tiles] * own.reshape(1, 1, 1)
        step = outer_rate * (clipped + momentum_rate * (decay_ref[tiles] + clipped))
        update[tiles] = step.astype(jnp.bfloat16)
        copies.append(pltpu.make_async_copy(update.at[tiles], update_out.at[tiles], sems.at[piece]))
        copies[-1].start()
    for m in range(modules):
        k = jnp.sum(jnp.where(lane[0:1, :] == 4 * m, shrink, 0.0), axis=1, keepdims=True)
        new[m] = momentum_rate * momentum_ref[m] + own_grad_ref[m] * k
    copies.append(pltpu.make_async_copy(new, new_out, sems.at[PIECES]))
    copies[-1].start()
    for copy in copies:
        copy.wait()


def local(deltas, momentum, path_module):
    modules, rows, width = momentum.shape
    columns = deltas.shape[2]
    peers = lax.axis_size(PATH)
    shards = lax.axis_size("shard")
    shape = jax.ShapeDtypeStruct
    tiles = deltas.reshape(2, 8, peers // 2, 128).transpose(0, 2, 1, 3).reshape(peers, 8, 128)
    column_tiles = lax.all_to_all(tiles, TILES, 0, 0, tiled=True)
    other = lax.ppermute(momentum, "path_2", [(0, 1), (1, 0)])
    module_tiles = shape((modules, 8, 128), jnp.float32)
    *packed, own = kernel(
        momentum_kernel,
        "pack_momentum",
        out_shape=(
            shape((modules, 8, 128), jnp.int32),
            shape((modules, 128), jnp.int32),
            module_tiles,
            shape((modules, 128), jnp.float32),
            shape((peers // PACKED, 128), jnp.int32),
            shape((1, 128), jnp.float32),
        ),
        in_specs=[SMEM, VMEM, VMEM],
        out_specs=(VMEM,) * 6,
        scratch_shapes=[pltpu.SMEM((modules,), jnp.int32)],
    )(path_module, momentum, other)
    chunks, grad = kernel(
        gather_kernel,
        "gather_modules",
        out_shape=(shape((peers * CHUNK, 128), jnp.int32), module_tiles),
        in_specs=[VMEM] * 6,
        out_specs=(VMEM, VMEM),
        scratch_shapes=[pltpu.VMEM((modules, 8, 128), jnp.float32)] * 4
        + [pltpu.VMEM((modules, 16, 128), jnp.int32)],
    )(column_tiles, *packed)
    chunks = lax.all_to_all(chunks.reshape(peers, CHUNK, 1, 128), TILES, 0, 0, tiled=True)
    squares = lax.shift_right_logical(chunks[:, UPPER], 24).astype(jnp.float32)
    squares = jnp.broadcast_to(jnp.sum(squares, axis=0), (shards, 1, 128))
    squares, grad = lax.optimization_barrier((squares, grad))
    squares = lax.all_to_all(squares, "shard", 0, 0, tiled=True)
    other = lax.ppermute(grad, "path_2", [(0, 1), (1, 0)])
    path_tiles = shape((peers, 8, 128), jnp.float32)
    *assembled, own = kernel(
        assemble_kernel,
        "assemble",
        out_shape=(path_tiles, path_tiles, shape((1, 128), jnp.float32)),
        in_specs=[VMEM] * 2,
        out_specs=(VMEM,) * 3,
        cost_estimate=pl.CostEstimate(flops=1 << 30, bytes_accessed=2 << 20, transcendentals=0),
    )(chunks.reshape(peers * CHUNK, 128), own)
    columns_grad, own = kernel(
        columns_kernel,
        "state_columns",
        out_shape=(shape(momentum.shape, jnp.float32), shape((1, 128), jnp.float32)),
        in_specs=[VMEM] * 3,
        out_specs=(VMEM,) * 2,
    )(grad, other, own)
    limit = clip_ratio * float(rows * shards * columns) ** 0.5
    update, new_momentum = kernel(
        lambda *refs: step_kernel(limit, *refs),
        "step",
        out_shape=(
            shape((peers, 8, 128), jnp.bfloat16),
            shape(momentum.shape, jnp.float32),
        ),
        in_specs=[VMEM] * 6,
        out_specs=(HBM, HBM),
        scratch_shapes=[
            pltpu.VMEM((peers, 8, 128), jnp.bfloat16),
            pltpu.VMEM(momentum.shape, jnp.float32),
            pltpu.SemaphoreType.DMA((PIECES + 1,)),
        ],
    )(
        squares.reshape(shards, 128),
        *assembled,
        columns_grad,
        own,
        momentum,
    )
    update = update.reshape(2, peers // 2, 8, 128).transpose(0, 2, 1, 3).reshape(deltas.shape)
    return (update, new_momentum)


def solution(mesh):
    finer = Mesh(
        mesh.devices.reshape(4, 8, 2, mesh.shape["shard"]), ("path_0", "path_1", "path_2", "shard")
    )
    in_specs = (P(PATH, "shard", None), P(None, "shard", PATH), P())
    out_specs = (P(PATH, "shard", None), P(None, "shard", PATH))
    return jax.shard_map(local, mesh=finer, in_specs=in_specs, out_specs=out_specs, check_vma=False)
```

```python
import jax
import jax.numpy as jnp
from jax import lax
from jax.experimental import pallas as pl
from jax.experimental.pallas import tpu as pltpu
from jax.sharding import Mesh
from jax.sharding import PartitionSpec as P

PATH = ("path_0", "path_1", "path_2")
TILES = ("path_2", "path_0", "path_1")

outer_rate = 0.7
momentum_rate = 0.9
clip_ratio = 2.0

UPPER, CHUNK = 8, 9
GRAD_BITS, LOWER_BITS = 18, 13
EXPONENTS, BIAS = 64, 128
MODULE_BITS, PACKED = 4, 8
MOMENTUM_SCALE = 8191.0
SQUARES_SCALE = 128.0
FOLD = momentum_rate * momentum_rate / (1.0 + momentum_rate)
KERNEL_BYTES = 4 << 20
VMEM = pl.BlockSpec(memory_space=pltpu.VMEM)
SMEM = pl.BlockSpec(memory_space=pltpu.SMEM)
HBM = pl.BlockSpec(memory_space=pl.ANY)
PIECES = 4


def path_of(peer, chips):
    return (peer % chips) * 2 + peer // chips


def kernel(body, name, **kwargs):
    params = pltpu.CompilerParams(vmem_limit_bytes=KERNEL_BYTES)
    return pl.pallas_call(body, name=name, compiler_params=params, **kwargs)


def lanes():
    return lax.broadcasted_iota(jnp.int32, (8, 128), 1)


def nearest(x):
    return jnp.floor(x + 0.5).astype(jnp.int32)


def momentum_kernel(
    module_ref, mine_ref, other_ref,
    lower_ref, upper_ref, fold_ref, count_ref, peer_ref, own_ref, count,
):
    peers, modules = module_ref.shape[0], mine_ref.shape[0]
    for m in range(modules):
        count[m] = 0
    for q in range(peers):
        count[module_ref[q]] += 1
    for word in range(peers // PACKED):
        packed = 0
        for k in range(PACKED):
            m = module_ref[path_of(word * PACKED + k, peers // 2)]
            packed = packed | (m << (k * MODULE_BITS))
        peer_ref[word : word + 1, :] = jnp.full((1, 128), packed)
    chip = lax.axis_index("path_0") * lax.axis_size("path_1") + lax.axis_index("path_1")
    module = module_ref[chip * 2 + lax.axis_index("path_2")]
    own_ref[...] = (lanes()[0:1, :] == 4 * module).astype(jnp.float32)
    first_core = lax.axis_index("path_2") == 0
    row = lax.broadcasted_iota(jnp.int32, (8, 128), 0)
    for m in range(modules):
        count_ref[m : m + 1, :] = jnp.full((1, 128), count[m].astype(jnp.float32))
        mine = jnp.where(first_core, mine_ref[m, 0:8, :], mine_ref[m, 8:16, :])
        other = jnp.where(first_core, other_ref[m, 0:8, :], other_ref[m, 8:16, :])
        momentum = jnp.concatenate(
            [jnp.where(first_core, mine, other), jnp.where(first_core, other, mine)], axis=1
        )
        whole = nearest(momentum * MOMENTUM_SCALE)
        fold_ref[m] = FOLD * (momentum - whole.astype(jnp.float32) * (1.0 / MOMENTUM_SCALE))
        whole += 32768
        lower_ref[m] = whole & ((1 << LOWER_BITS) - 1)
        word = (whole >> LOWER_BITS) << (row * 3)
        for rows in (4, 2, 1):
            word = word | pltpu.roll(word, rows, 0)
        upper_ref[m : m + 1, :] = word[0:1, :]


def gather_kernel(
    column_ref, lower_ref, upper_ref, fold_ref, count_ref, peer_ref, chunk_ref, grad_ref, *scratch
):
    *sums, words = scratch
    peers, modules = column_ref.shape[0], grad_ref.shape[0]
    packed = [peer_ref[word, 0] for word in range(peers // PACKED)]
    module_of = [
        (packed[q // PACKED] >> (q % PACKED * MODULE_BITS)) & (2**MODULE_BITS - 1)
        for q in range(peers)
    ]
    for total in sums:
        total[...] = jnp.zeros_like(total)
    for q in range(peers):
        m = module_of[q]
        total = sums[q % len(sums)]
        total[m] += column_ref[q].astype(jnp.float32)
    for m in range(modules):
        total = sums[0][m]
        for more in sums[1:]:
            total += more[m]
        grad_ref[m] = total / count_ref[m : m + 1, :]
    grad = grad_ref[...]
    squares = jnp.sum(jnp.sum(grad * grad, axis=1), axis=1, keepdims=True)
    squares = nearest(squares * SQUARES_SCALE)
    row = lax.broadcasted_iota(jnp.int32, (modules, 128), 0)
    lane = lax.broadcasted_iota(jnp.int32, (modules, 128), 1)
    norms = jnp.where(lane >> 2 == row, (squares >> ((lane & 3) * 8)) & 255, 0)
    norms = jnp.sum(norms.astype(jnp.float32), axis=0, keepdims=True)
    limit = 2.0**GRAD_BITS - 1.0
    own_lane = lanes() == EXPONENTS + lax.broadcasted_iota(jnp.int32, (8, 128), 0)
    for m in range(modules):
        exact = grad_ref[m] + fold_ref[m]
        largest = jnp.max(jnp.abs(exact), axis=1, keepdims=True)
        power = jnp.ceil(jnp.log2(jnp.maximum(largest, 1e-30)))
        exact = jnp.clip(exact * jnp.exp2(GRAD_BITS - power), -limit, limit)
        words[m, 0:UPPER, :] = (nearest(exact) << LOWER_BITS) | lower_ref[m]
        powers = jnp.sum(jnp.where(own_lane, power + BIAS, 0.0), axis=0, keepdims=True)
        words[m, UPPER:CHUNK, :] = upper_ref[m : m + 1, :] | ((norms + powers).astype(jnp.int32) << 24)
    for path in range(peers):
        m = module_of[path % 2 * (peers // 2) + path // 2]
        start = path * CHUNK
        chunk_ref[start : start + UPPER, :] = words[m, 0:UPPER, :]
        chunk_ref[start + UPPER : start + CHUNK, :] = words[m, UPPER:CHUNK, :]


def assemble_kernel(chunk_ref, own_ref, grad_ref, decay_ref, mask_ref):
    peers = grad_ref.shape[0]
    power = lax.shift_right_logical(chunk_ref[pl.ds(UPPER, peers, stride=CHUNK), :], 24)
    scale = 1.0 / jnp.exp2(GRAD_BITS + BIAS - power.astype(jnp.float32))
    row = lax.broadcasted_iota(jnp.int32, (8, 128), 0)
    own_lane = lanes() == EXPONENTS + row
    for q in range(peers):
        path = path_of(q, peers // 2)
        start = path * CHUNK
        words = chunk_ref[start : start + UPPER, :]
        of_row = jnp.where(own_lane, scale[path : path + 1, :], 0.0)
        of_row = jnp.sum(of_row, axis=1, keepdims=True)
        grad_ref[q] = (words >> LOWER_BITS).astype(jnp.float32) * of_row
        upper = (chunk_ref[start + UPPER : start + CHUNK, :] >> (row * 3)) & 7
        whole = ((upper << LOWER_BITS) | (words & ((1 << LOWER_BITS) - 1))) - 32768
        decay_ref[q] = whole.astype(jnp.float32) * (momentum_rate / MOMENTUM_SCALE)
    mask_ref[...] = own_ref[...]


def columns_kernel(mine_ref, other_ref, mask_ref, grad_ref, own_ref):
    core = lax.axis_index("path_2")
    for m in range(mine_ref.shape[0]):
        for half in range(2):
            grad = jnp.where(core == half, mine_ref[m], other_ref[m])
            grad = jnp.where(core == 0, grad, pltpu.roll(grad, 64, 1))
            grad_ref[m, half * 8 : half * 8 + 8, :] = grad[:, 0:64]
    own_ref[...] = mask_ref[...]


def step_kernel(
    limit, squares_ref, grad_ref, decay_ref, own_grad_ref, own_ref, momentum_ref,
    update_out, new_out, update, new, sems,
):
    peers, modules = update.shape[0], new.shape[0]
    lane = lanes()
    norm_squares = jnp.broadcast_to(jnp.sum(squares_ref[...], axis=0, keepdims=True), (8, 128))
    for byte in range(4):
        weight = 256.0**byte / SQUARES_SCALE
        norm_squares = jnp.where(lane & 3 == byte, norm_squares * weight, norm_squares)
    norm_squares += pltpu.roll(norm_squares, 127, 1)
    norm_squares = (norm_squares + pltpu.roll(norm_squares, 126, 1))[0:1, :]
    shrink = jnp.minimum(1.0, limit / jnp.sqrt(norm_squares + 1e-06))
    own = jnp.sum(jnp.where(own_ref[...] > 0.0, shrink, 0.0), axis=1, keepdims=True)
    each = peers // PIECES
    copies = []
    for piece in range(PIECES):
        tiles = slice(piece * each, (piece + 1) * each)
        clipped = grad_ref[tiles] * own.reshape(1, 1, 1)
        step = outer_rate * (clipped + momentum_rate * (decay_ref[tiles] + clipped))
        update[tiles] = step.astype(jnp.bfloat16)
        copies.append(pltpu.make_async_copy(update.at[tiles], update_out.at[tiles], sems.at[piece]))
        copies[-1].start()
    for m in range(modules):
        k = jnp.sum(jnp.where(lane[0:1, :] == 4 * m, shrink, 0.0), axis=1, keepdims=True)
        new[m] = momentum_rate * momentum_ref[m] + own_grad_ref[m] * k
    copies.append(pltpu.make_async_copy(new, new_out, sems.at[PIECES]))
    copies[-1].start()
    for copy in copies:
        copy.wait()


def local(deltas, momentum, path_module):
    modules, rows, width = momentum.shape
    columns = deltas.shape[2]
    peers = lax.axis_size(PATH)
    shards = lax.axis_size("shard")
    shape = jax.ShapeDtypeStruct
    tiles = deltas.reshape(2, 8, peers // 2, 128).transpose(0, 2, 1, 3).reshape(peers, 8, 128)
    column_tiles = lax.all_to_all(tiles, TILES, 0, 0, tiled=True)
    other = lax.ppermute(momentum, "path_2", [(0, 1), (1, 0)])
    module_tiles = shape((modules, 8, 128), jnp.float32)
    *packed, own = kernel(
        momentum_kernel,
        "pack_momentum",
        out_shape=(
            shape((modules, 8, 128), jnp.int32),
            shape((modules, 128), jnp.int32),
            module_tiles,
            shape((modules, 128), jnp.float32),
            shape((peers // PACKED, 128), jnp.int32),
            shape((1, 128), jnp.float32),
        ),
        in_specs=[SMEM, VMEM, VMEM],
        out_specs=(VMEM,) * 6,
        scratch_shapes=[pltpu.SMEM((modules,), jnp.int32)],
    )(path_module, momentum, other)
    chunks, grad = kernel(
        gather_kernel,
        "gather_modules",
        out_shape=(shape((peers * CHUNK, 128), jnp.int32), module_tiles),
        in_specs=[VMEM] * 6,
        out_specs=(VMEM, VMEM),
        scratch_shapes=[pltpu.VMEM((modules, 8, 128), jnp.float32)] * 4
        + [pltpu.VMEM((modules, 16, 128), jnp.int32)],
    )(column_tiles, *packed)
    chunks = lax.all_to_all(chunks.reshape(peers, CHUNK, 1, 128), PATH, 0, 0, tiled=True)
    squares = lax.shift_right_logical(chunks[:, UPPER], 24).astype(jnp.float32)
    squares = jnp.broadcast_to(jnp.sum(squares, axis=0), (shards, 1, 128))
    squares, grad = lax.optimization_barrier((squares, grad))
    squares = lax.all_to_all(squares, "shard", 0, 0, tiled=True)
    other = lax.ppermute(grad, "path_2", [(0, 1), (1, 0)])
    path_tiles = shape((peers, 8, 128), jnp.float32)
    *assembled, own = kernel(
        assemble_kernel,
        "assemble",
        out_shape=(path_tiles, path_tiles, shape((1, 128), jnp.float32)),
        in_specs=[VMEM] * 2,
        out_specs=(VMEM,) * 3,
        cost_estimate=pl.CostEstimate(flops=1 << 30, bytes_accessed=2 << 20, transcendentals=0),
    )(chunks.reshape(peers * CHUNK, 128), own)
    columns_grad, own = kernel(
        columns_kernel,
        "state_columns",
        out_shape=(shape(momentum.shape, jnp.float32), shape((1, 128), jnp.float32)),
        in_specs=[VMEM] * 3,
        out_specs=(VMEM,) * 2,
    )(grad, other, own)
    limit = clip_ratio * float(rows * shards * columns) ** 0.5
    update, new_momentum = kernel(
        lambda *refs: step_kernel(limit, *refs),
        "step",
        out_shape=(
            shape((peers, 8, 128), jnp.bfloat16),
            shape(momentum.shape, jnp.float32),
        ),
        in_specs=[VMEM] * 6,
        out_specs=(HBM, HBM),
        scratch_shapes=[
            pltpu.VMEM((peers, 8, 128), jnp.bfloat16),
            pltpu.VMEM(momentum.shape, jnp.float32),
            pltpu.SemaphoreType.DMA((PIECES + 1,)),
        ],
    )(
        squares.reshape(shards, 128),
        *assembled,
        columns_grad,
        own,
        momentum,
    )
    update = update.reshape(2, peers // 2, 8, 128).transpose(0, 2, 1, 3).reshape(deltas.shape)
    return (update, new_momentum)


def solution(mesh):
    finer = Mesh(
        mesh.devices.reshape(4, 8, 2, mesh.shape["shard"]), ("path_0", "path_1", "path_2", "shard")
    )
    in_specs = (P(PATH, "shard", None), P(None, "shard", PATH), P())
    out_specs = (P(PATH, "shard", None), P(None, "shard", PATH))
    return jax.shard_map(local, mesh=finer, in_specs=in_specs, out_specs=out_specs, check_vma=False)
```

```python
import jax
import jax.numpy as jnp
from jax import lax
from jax.experimental import pallas as pl
from jax.experimental.pallas import tpu as pltpu
from jax.sharding import Mesh
from jax.sharding import PartitionSpec as P

PATH = ("path_0", "path_1", "path_2")
TILES = ("path_2", "path_0", "path_1")

SHARD = ("shard_2", "shard_1", "shard_0")
SHARD_ORDER = ("shard_1", "shard_2", "shard_0")

outer_rate = 0.7
momentum_rate = 0.9
clip_ratio = 2.0

UPPER, CHUNK = 8, 9
GRAD_BITS, LOWER_BITS = 18, 13
EXPONENTS, BIAS = 64, 128
MODULE_BITS, PACKED = 4, 8
MOMENTUM_SCALE = 8191.0
SQUARES_SCALE = 128.0
FOLD = momentum_rate * momentum_rate / (1.0 + momentum_rate)
KERNEL_BYTES = 4 << 20
VMEM = pl.BlockSpec(memory_space=pltpu.VMEM)
SMEM = pl.BlockSpec(memory_space=pltpu.SMEM)
HBM = pl.BlockSpec(memory_space=pl.ANY)
PIECES = 4


def path_of(peer, chips):
    return (peer % chips) * 2 + peer // chips


def kernel(body, name, **kwargs):
    params = pltpu.CompilerParams(vmem_limit_bytes=KERNEL_BYTES)
    return pl.pallas_call(body, name=name, compiler_params=params, **kwargs)


def lanes():
    return lax.broadcasted_iota(jnp.int32, (8, 128), 1)


def nearest(x):
    return jnp.floor(x + 0.5).astype(jnp.int32)


def momentum_kernel(
    module_ref, mine_ref, other_ref,
    lower_ref, upper_ref, fold_ref, count_ref, peer_ref, own_ref, count,
):
    peers, modules = module_ref.shape[0], mine_ref.shape[0]
    for m in range(modules):
        count[m] = 0
    for q in range(peers):
        count[module_ref[q]] += 1
    for word in range(peers // PACKED):
        packed = 0
        for k in range(PACKED):
            m = module_ref[path_of(word * PACKED + k, peers // 2)]
            packed = packed | (m << (k * MODULE_BITS))
        peer_ref[word : word + 1, :] = jnp.full((1, 128), packed)
    chip = lax.axis_index("path_0") * lax.axis_size("path_1") + lax.axis_index("path_1")
    module = module_ref[chip * 2 + lax.axis_index("path_2")]
    own_ref[...] = (lanes()[0:1, :] == 4 * module).astype(jnp.float32)
    first_core = lax.axis_index("path_2") == 0
    row = lax.broadcasted_iota(jnp.int32, (8, 128), 0)
    for m in range(modules):
        count_ref[m : m + 1, :] = jnp.full((1, 128), count[m].astype(jnp.float32))
        mine = jnp.where(first_core, mine_ref[m, 0:8, :], mine_ref[m, 8:16, :])
        other = jnp.where(first_core, other_ref[m, 0:8, :], other_ref[m, 8:16, :])
        momentum = jnp.concatenate(
            [jnp.where(first_core, mine, other), jnp.where(first_core, other, mine)], axis=1
        )
        whole = nearest(momentum * MOMENTUM_SCALE)
        fold_ref[m] = FOLD * (momentum - whole.astype(jnp.float32) * (1.0 / MOMENTUM_SCALE))
        whole += 32768
        lower_ref[m] = whole & ((1 << LOWER_BITS) - 1)
        word = (whole >> LOWER_BITS) << (row * 3)
        for rows in (4, 2, 1):
            word = word | pltpu.roll(word, rows, 0)
        upper_ref[m : m + 1, :] = word[0:1, :]


def gather_kernel(
    column_ref, lower_ref, upper_ref, fold_ref, count_ref, peer_ref, chunk_ref, grad_ref, *scratch
):
    *sums, words = scratch
    peers, modules = column_ref.shape[0], grad_ref.shape[0]
    packed = [peer_ref[word, 0] for word in range(peers // PACKED)]
    module_of = [
        (packed[q // PACKED] >> (q % PACKED * MODULE_BITS)) & (2**MODULE_BITS - 1)
        for q in range(peers)
    ]
    for total in sums:
        total[...] = jnp.zeros_like(total)
    for q in range(peers):
        m = module_of[q]
        total = sums[q % len(sums)]
        total[m] += column_ref[q].astype(jnp.float32)
    for m in range(modules):
        total = sums[0][m]
        for more in sums[1:]:
            total += more[m]
        grad_ref[m] = total / count_ref[m : m + 1, :]
    grad = grad_ref[...]
    squares = jnp.sum(jnp.sum(grad * grad, axis=1), axis=1, keepdims=True)
    squares = nearest(squares * SQUARES_SCALE)
    row = lax.broadcasted_iota(jnp.int32, (modules, 128), 0)
    lane = lax.broadcasted_iota(jnp.int32, (modules, 128), 1)
    norms = jnp.where(lane >> 2 == row, (squares >> ((lane & 3) * 8)) & 255, 0)
    norms = jnp.sum(norms.astype(jnp.float32), axis=0, keepdims=True)
    limit = 2.0**GRAD_BITS - 1.0
    own_lane = lanes() == EXPONENTS + lax.broadcasted_iota(jnp.int32, (8, 128), 0)
    for m in range(modules):
        exact = grad_ref[m] + fold_ref[m]
        largest = jnp.max(jnp.abs(exact), axis=1, keepdims=True)
        power = jnp.ceil(jnp.log2(jnp.maximum(largest, 1e-30)))
        exact = jnp.clip(exact * jnp.exp2(GRAD_BITS - power), -limit, limit)
        words[m, 0:UPPER, :] = (nearest(exact) << LOWER_BITS) | lower_ref[m]
        powers = jnp.sum(jnp.where(own_lane, power + BIAS, 0.0), axis=0, keepdims=True)
        words[m, UPPER:CHUNK, :] = upper_ref[m : m + 1, :] | ((norms + powers).astype(jnp.int32) << 24)
    for path in range(peers):
        m = module_of[path % 2 * (peers // 2) + path // 2]
        start = path * CHUNK
        chunk_ref[start : start + UPPER, :] = words[m, 0:UPPER, :]
        chunk_ref[start + UPPER : start + CHUNK, :] = words[m, UPPER:CHUNK, :]


def squares_kernel(chunk_ref, squares_out, squares, sem):
    peers = chunk_ref.shape[0] // CHUNK
    norms = lax.shift_right_logical(chunk_ref[pl.ds(UPPER, peers, stride=CHUNK), :], 24)
    norms = jnp.sum(norms.astype(jnp.float32), axis=0, keepdims=True)
    squares[...] = jnp.broadcast_to(norms, squares.shape)
    copy = pltpu.make_async_copy(squares, squares_out, sem)
    copy.start()
    copy.wait()


def assemble_kernel(chunk_ref, own_ref, grad_ref, decay_ref, mask_ref):
    peers = grad_ref.shape[0]
    power = lax.shift_right_logical(chunk_ref[pl.ds(UPPER, peers, stride=CHUNK), :], 24)
    scale = 1.0 / jnp.exp2(GRAD_BITS + BIAS - power.astype(jnp.float32))
    row = lax.broadcasted_iota(jnp.int32, (8, 128), 0)
    own_lane = lanes() == EXPONENTS + row
    for q in range(peers):
        path = path_of(q, peers // 2)
        start = path * CHUNK
        words = chunk_ref[start : start + UPPER, :]
        of_row = jnp.where(own_lane, scale[path : path + 1, :], 0.0)
        of_row = jnp.sum(of_row, axis=1, keepdims=True)
        grad_ref[q] = (words >> LOWER_BITS).astype(jnp.float32) * of_row
        upper = (chunk_ref[start + UPPER : start + CHUNK, :] >> (row * 3)) & 7
        whole = ((upper << LOWER_BITS) | (words & ((1 << LOWER_BITS) - 1))) - 32768
        decay_ref[q] = whole.astype(jnp.float32) * (momentum_rate / MOMENTUM_SCALE)
    mask_ref[...] = own_ref[...]


def columns_kernel(mine_ref, other_ref, mask_ref, grad_ref, own_ref):
    core = lax.axis_index("path_2")
    for m in range(mine_ref.shape[0]):
        for half in range(2):
            grad = jnp.where(core == half, mine_ref[m], other_ref[m])
            grad = jnp.where(core == 0, grad, pltpu.roll(grad, 64, 1))
            grad_ref[m, half * 8 : half * 8 + 8, :] = grad[:, 0:64]
    own_ref[...] = mask_ref[...]


def step_kernel(
    limit, squares_ref, grad_ref, decay_ref, own_grad_ref, own_ref, momentum_ref,
    update_out, new_out, update, new, sems,
):
    peers, modules = update.shape[0], new.shape[0]
    lane = lanes()
    norm_squares = jnp.broadcast_to(jnp.sum(squares_ref[...], axis=0, keepdims=True), (8, 128))
    for byte in range(4):
        weight = 256.0**byte / SQUARES_SCALE
        norm_squares = jnp.where(lane & 3 == byte, norm_squares * weight, norm_squares)
    norm_squares += pltpu.roll(norm_squares, 127, 1)
    norm_squares = (norm_squares + pltpu.roll(norm_squares, 126, 1))[0:1, :]
    shrink = jnp.minimum(1.0, limit / jnp.sqrt(norm_squares + 1e-06))
    own = jnp.sum(jnp.where(own_ref[...] > 0.0, shrink, 0.0), axis=1, keepdims=True)
    each = peers // PIECES
    copies = []
    for piece in range(PIECES):
        tiles = slice(piece * each, (piece + 1) * each)
        clipped = grad_ref[tiles] * own.reshape(1, 1, 1)
        step = outer_rate * (clipped + momentum_rate * (decay_ref[tiles] + clipped))
        update[tiles] = step.astype(jnp.bfloat16)
        copies.append(pltpu.make_async_copy(update.at[tiles], update_out.at[tiles], sems.at[piece]))
        copies[-1].start()
    for m in range(modules):
        k = jnp.sum(jnp.where(lane[0:1, :] == 4 * m, shrink, 0.0), axis=1, keepdims=True)
        new[m] = momentum_rate * momentum_ref[m] + own_grad_ref[m] * k
    copies.append(pltpu.make_async_copy(new, new_out, sems.at[PIECES]))
    copies[-1].start()
    for copy in copies:
        copy.wait()


def local(deltas, momentum, path_module):
    modules, rows, width = momentum.shape
    columns = deltas.shape[2]
    peers = lax.axis_size(PATH)
    shards = lax.axis_size(SHARD)
    shape = jax.ShapeDtypeStruct
    tiles = deltas.reshape(2, 8, peers // 2, 128).transpose(0, 2, 1, 3).reshape(peers, 8, 128)
    column_tiles = lax.all_to_all(tiles, TILES, 0, 0, tiled=True)
    other = lax.ppermute(momentum, "path_2", [(0, 1), (1, 0)])
    module_tiles = shape((modules, 8, 128), jnp.float32)
    *packed, own = kernel(
        momentum_kernel,
        "pack_momentum",
        out_shape=(
            shape((modules, 8, 128), jnp.int32),
            shape((modules, 128), jnp.int32),
            module_tiles,
            shape((modules, 128), jnp.float32),
            shape((peers // PACKED, 128), jnp.int32),
            shape((1, 128), jnp.float32),
        ),
        in_specs=[SMEM, VMEM, VMEM],
        out_specs=(VMEM,) * 6,
        scratch_shapes=[pltpu.SMEM((modules,), jnp.int32)],
    )(path_module, momentum, other)
    chunks, grad = kernel(
        gather_kernel,
        "gather_modules",
        out_shape=(shape((peers * CHUNK, 128), jnp.int32), module_tiles),
        in_specs=[VMEM] * 6,
        out_specs=(VMEM, VMEM),
        scratch_shapes=[pltpu.VMEM((modules, 8, 128), jnp.float32)] * 4
        + [pltpu.VMEM((modules, 16, 128), jnp.int32)],
    )(column_tiles, *packed)
    chunks = lax.all_to_all(chunks.reshape(peers, CHUNK, 1, 128), PATH, 0, 0, tiled=True)
    chunks = chunks.reshape(peers * CHUNK, 128)
    squares = kernel(
        squares_kernel,
        "sum_squares",
        out_shape=shape((shards, 128), jnp.float32),
        in_specs=[VMEM],
        out_specs=HBM,
        scratch_shapes=[pltpu.VMEM((shards, 128), jnp.float32), pltpu.SemaphoreType.DMA],
    )(chunks)
    squares = squares.reshape(shards, 1, 128)
    squares, grad = lax.optimization_barrier((squares, grad))
    squares = lax.all_to_all(squares, SHARD_ORDER, 0, 0, tiled=True)
    other = lax.ppermute(grad, "path_2", [(0, 1), (1, 0)])
    path_tiles = shape((peers, 8, 128), jnp.float32)
    *assembled, own = kernel(
        assemble_kernel,
        "assemble",
        out_shape=(path_tiles, path_tiles, shape((1, 128), jnp.float32)),
        in_specs=[VMEM] * 2,
        out_specs=(VMEM,) * 3,
        cost_estimate=pl.CostEstimate(flops=1 << 30, bytes_accessed=2 << 20, transcendentals=0),
    )(chunks, own)
    columns_grad, own = kernel(
        columns_kernel,
        "state_columns",
        out_shape=(shape(momentum.shape, jnp.float32), shape((1, 128), jnp.float32)),
        in_specs=[VMEM] * 3,
        out_specs=(VMEM,) * 2,
    )(grad, other, own)
    limit = clip_ratio * float(rows * shards * columns) ** 0.5
    update, new_momentum = kernel(
        lambda *refs: step_kernel(limit, *refs),
        "step",
        out_shape=(
            shape((peers, 8, 128), jnp.bfloat16),
            shape(momentum.shape, jnp.float32),
        ),
        in_specs=[VMEM] * 6,
        out_specs=(HBM, HBM),
        scratch_shapes=[
            pltpu.VMEM((peers, 8, 128), jnp.bfloat16),
            pltpu.VMEM(momentum.shape, jnp.float32),
            pltpu.SemaphoreType.DMA((PIECES + 1,)),
        ],
    )(
        squares.reshape(shards, 128),
        *assembled,
        columns_grad,
        own,
        momentum,
    )
    update = update.reshape(2, peers // 2, 8, 128).transpose(0, 2, 1, 3).reshape(deltas.shape)
    return (update, new_momentum)


def solution(mesh):
    finer = Mesh(
        mesh.devices.reshape(4, 8, 2, 2, 2, 2), (*PATH, *SHARD)
    )
    in_specs = (P(PATH, SHARD, None), P(None, SHARD, PATH), P())
    out_specs = (P(PATH, SHARD, None), P(None, SHARD, PATH))
    return jax.shard_map(local, mesh=finer, in_specs=in_specs, out_specs=out_specs, check_vma=False)
```

```python
import jax
import jax.numpy as jnp
from jax import lax
from jax.experimental import pallas as pl
from jax.experimental.pallas import tpu as pltpu
from jax.sharding import Mesh
from jax.sharding import PartitionSpec as P

PATH = ("path_0", "path_1", "path_2")
TILES = ("path_2", "path_0", "path_1")

SHARD = ("shard_2", "shard_1", "shard_0")
SHARD_ORDER = ("shard_1", "shard_2", "shard_0")

outer_rate = 0.7
momentum_rate = 0.9
clip_ratio = 2.0

UPPER, CHUNK = 8, 9
GRAD_BITS, LOWER_BITS = 18, 13
EXPONENTS, BIAS = 64, 128
MODULE_BITS, PACKED = 4, 8
MOMENTUM_SCALE = 8191.0
SQUARES_SCALE = 128.0
FOLD = momentum_rate * momentum_rate / (1.0 + momentum_rate)
KERNEL_BYTES = 4 << 20
VMEM = pl.BlockSpec(memory_space=pltpu.VMEM)
SMEM = pl.BlockSpec(memory_space=pltpu.SMEM)
HBM = pl.BlockSpec(memory_space=pl.ANY)
PIECES = 4


def path_of(peer, chips):
    return (peer % chips) * 2 + peer // chips


def kernel(body, name, **kwargs):
    params = pltpu.CompilerParams(vmem_limit_bytes=KERNEL_BYTES)
    return pl.pallas_call(body, name=name, compiler_params=params, **kwargs)


def lanes():
    return lax.broadcasted_iota(jnp.int32, (8, 128), 1)


def nearest(x):
    return jnp.floor(x + 0.5).astype(jnp.int32)


def momentum_kernel(
    module_ref, mine_ref, other_ref,
    lower_ref, upper_ref, fold_ref, count_ref, peer_ref, own_ref, count,
):
    peers, modules = module_ref.shape[0], mine_ref.shape[0]
    for m in range(modules):
        count[m] = 0
    for q in range(peers):
        count[module_ref[q]] += 1
    for word in range(peers // PACKED):
        packed = 0
        for k in range(PACKED):
            m = module_ref[path_of(word * PACKED + k, peers // 2)]
            packed = packed | (m << (k * MODULE_BITS))
        peer_ref[word : word + 1, :] = jnp.full((1, 128), packed)
    chip = lax.axis_index("path_0") * lax.axis_size("path_1") + lax.axis_index("path_1")
    module = module_ref[chip * 2 + lax.axis_index("path_2")]
    own_ref[...] = (lanes()[0:1, :] == 4 * module).astype(jnp.float32)
    first_core = lax.axis_index("path_2") == 0
    row = lax.broadcasted_iota(jnp.int32, (8, 128), 0)
    for m in range(modules):
        count_ref[m : m + 1, :] = jnp.full((1, 128), count[m].astype(jnp.float32))
        mine = jnp.where(first_core, mine_ref[m, 0:8, :], mine_ref[m, 8:16, :])
        other = other_ref[m]
        momentum = jnp.concatenate(
            [jnp.where(first_core, mine, other), jnp.where(first_core, other, mine)], axis=1
        )
        whole = nearest(momentum * MOMENTUM_SCALE)
        fold_ref[m] = FOLD * (momentum - whole.astype(jnp.float32) * (1.0 / MOMENTUM_SCALE))
        whole += 32768
        lower_ref[m] = whole & ((1 << LOWER_BITS) - 1)
        word = (whole >> LOWER_BITS) << (row * 3)
        for rows in (4, 2, 1):
            word = word | pltpu.roll(word, rows, 0)
        upper_ref[m : m + 1, :] = word[0:1, :]


def gather_kernel(
    column_ref, lower_ref, upper_ref, fold_ref, count_ref, peer_ref, chunk_ref, grad_ref, *scratch
):
    *sums, words = scratch
    peers, modules = column_ref.shape[0], grad_ref.shape[0]
    packed = [peer_ref[word, 0] for word in range(peers // PACKED)]
    module_of = [
        (packed[q // PACKED] >> (q % PACKED * MODULE_BITS)) & (2**MODULE_BITS - 1)
        for q in range(peers)
    ]
    for total in sums:
        total[...] = jnp.zeros_like(total)
    for q in range(peers):
        m = module_of[q]
        total = sums[q % len(sums)]
        total[m] += column_ref[q].astype(jnp.float32)
    for m in range(modules):
        total = sums[0][m]
        for more in sums[1:]:
            total += more[m]
        grad_ref[m] = total / count_ref[m : m + 1, :]
    grad = grad_ref[...]
    squares = jnp.sum(jnp.sum(grad * grad, axis=1), axis=1, keepdims=True)
    squares = nearest(squares * SQUARES_SCALE)
    row = lax.broadcasted_iota(jnp.int32, (modules, 128), 0)
    lane = lax.broadcasted_iota(jnp.int32, (modules, 128), 1)
    norms = jnp.where(lane >> 2 == row, (squares >> ((lane & 3) * 8)) & 255, 0)
    norms = jnp.sum(norms.astype(jnp.float32), axis=0, keepdims=True)
    limit = 2.0**GRAD_BITS - 1.0
    own_lane = lanes() == EXPONENTS + lax.broadcasted_iota(jnp.int32, (8, 128), 0)
    for m in range(modules):
        exact = grad_ref[m] + fold_ref[m]
        largest = jnp.max(jnp.abs(exact), axis=1, keepdims=True)
        power = jnp.ceil(jnp.log2(jnp.maximum(largest, 1e-30)))
        exact = jnp.clip(exact * jnp.exp2(GRAD_BITS - power), -limit, limit)
        words[m, 0:UPPER, :] = (nearest(exact) << LOWER_BITS) | lower_ref[m]
        powers = jnp.sum(jnp.where(own_lane, power + BIAS, 0.0), axis=0, keepdims=True)
        words[m, UPPER:CHUNK, :] = upper_ref[m : m + 1, :] | ((norms + powers).astype(jnp.int32) << 24)
    for path in range(peers):
        m = module_of[path % 2 * (peers // 2) + path // 2]
        start = path * CHUNK
        chunk_ref[start : start + UPPER, :] = words[m, 0:UPPER, :]
        chunk_ref[start + UPPER : start + CHUNK, :] = words[m, UPPER:CHUNK, :]


def squares_kernel(chunk_ref, squares_out, squares, sem):
    peers = chunk_ref.shape[0] // CHUNK
    norms = lax.shift_right_logical(chunk_ref[pl.ds(UPPER, peers, stride=CHUNK), :], 24)
    norms = jnp.sum(norms.astype(jnp.float32), axis=0, keepdims=True)
    squares[...] = jnp.broadcast_to(norms, squares.shape)
    copy = pltpu.make_async_copy(squares, squares_out, sem)
    copy.start()
    copy.wait()


def assemble_kernel(chunk_ref, own_ref, grad_ref, decay_ref, mask_ref):
    peers = grad_ref.shape[0]
    power = lax.shift_right_logical(chunk_ref[pl.ds(UPPER, peers, stride=CHUNK), :], 24)
    scale = 1.0 / jnp.exp2(GRAD_BITS + BIAS - power.astype(jnp.float32))
    row = lax.broadcasted_iota(jnp.int32, (8, 128), 0)
    own_lane = lanes() == EXPONENTS + row
    for q in range(peers):
        path = path_of(q, peers // 2)
        start = path * CHUNK
        words = chunk_ref[start : start + UPPER, :]
        of_row = jnp.where(own_lane, scale[path : path + 1, :], 0.0)
        of_row = jnp.sum(of_row, axis=1, keepdims=True)
        grad_ref[q] = (words >> LOWER_BITS).astype(jnp.float32) * of_row
        upper = (chunk_ref[start + UPPER : start + CHUNK, :] >> (row * 3)) & 7
        whole = ((upper << LOWER_BITS) | (words & ((1 << LOWER_BITS) - 1))) - 32768
        decay_ref[q] = whole.astype(jnp.float32) * (momentum_rate / MOMENTUM_SCALE)
    mask_ref[...] = own_ref[...]


def columns_kernel(mine_ref, other_ref, mask_ref, grad_ref, own_ref):
    core = lax.axis_index("path_2")
    for m in range(mine_ref.shape[0]):
        for half in range(2):
            grad = jnp.where(core == half, mine_ref[m], other_ref[m])
            grad = jnp.where(core == 0, grad, pltpu.roll(grad, 64, 1))
            grad_ref[m, half * 8 : half * 8 + 8, :] = grad[:, 0:64]
    own_ref[...] = mask_ref[...]


def step_kernel(
    limit, squares_ref, grad_ref, decay_ref, own_grad_ref, own_ref, momentum_ref,
    update_out, new_out, update, new, sems,
):
    peers, modules = update.shape[0], new.shape[0]
    lane = lanes()
    norm_squares = jnp.broadcast_to(jnp.sum(squares_ref[...], axis=0, keepdims=True), (8, 128))
    for byte in range(4):
        weight = 256.0**byte / SQUARES_SCALE
        norm_squares = jnp.where(lane & 3 == byte, norm_squares * weight, norm_squares)
    norm_squares += pltpu.roll(norm_squares, 127, 1)
    norm_squares = (norm_squares + pltpu.roll(norm_squares, 126, 1))[0:1, :]
    shrink = jnp.minimum(1.0, limit / jnp.sqrt(norm_squares + 1e-06))
    own = jnp.sum(jnp.where(own_ref[...] > 0.0, shrink, 0.0), axis=1, keepdims=True)
    each = peers // PIECES
    copies = []
    for piece in range(PIECES):
        tiles = slice(piece * each, (piece + 1) * each)
        clipped = grad_ref[tiles] * own.reshape(1, 1, 1)
        step = outer_rate * (clipped + momentum_rate * (decay_ref[tiles] + clipped))
        update[tiles] = step.astype(jnp.bfloat16)
        copies.append(pltpu.make_async_copy(update.at[tiles], update_out.at[tiles], sems.at[piece]))
        copies[-1].start()
    for m in range(modules):
        k = jnp.sum(jnp.where(lane[0:1, :] == 4 * m, shrink, 0.0), axis=1, keepdims=True)
        new[m] = momentum_rate * momentum_ref[m] + own_grad_ref[m] * k
    copies.append(pltpu.make_async_copy(new, new_out, sems.at[PIECES]))
    copies[-1].start()
    for copy in copies:
        copy.wait()


def local(deltas, momentum, path_module):
    modules, rows, width = momentum.shape
    columns = deltas.shape[2]
    peers = lax.axis_size(PATH)
    shards = lax.axis_size(SHARD)
    shape = jax.ShapeDtypeStruct
    tiles = deltas.reshape(2, 8, peers // 2, 128).transpose(0, 2, 1, 3).reshape(peers, 8, 128)
    column_tiles = lax.all_to_all(tiles, TILES, 0, 0, tiled=True)
    half = jnp.where(lax.axis_index("path_2") == 0, momentum[:, 8:16], momentum[:, 0:8])
    other = lax.ppermute(half, "path_2", [(0, 1), (1, 0)])
    module_tiles = shape((modules, 8, 128), jnp.float32)
    *packed, own = kernel(
        momentum_kernel,
        "pack_momentum",
        out_shape=(
            shape((modules, 8, 128), jnp.int32),
            shape((modules, 128), jnp.int32),
            module_tiles,
            shape((modules, 128), jnp.float32),
            shape((peers // PACKED, 128), jnp.int32),
            shape((1, 128), jnp.float32),
        ),
        in_specs=[SMEM, VMEM, VMEM],
        out_specs=(VMEM,) * 6,
        scratch_shapes=[pltpu.SMEM((modules,), jnp.int32)],
    )(path_module, momentum, other)
    chunks, grad = kernel(
        gather_kernel,
        "gather_modules",
        out_shape=(shape((peers * CHUNK, 128), jnp.int32), module_tiles),
        in_specs=[VMEM] * 6,
        out_specs=(VMEM, VMEM),
        scratch_shapes=[pltpu.VMEM((modules, 8, 128), jnp.float32)] * 4
        + [pltpu.VMEM((modules, 16, 128), jnp.int32)],
    )(column_tiles, *packed)
    chunks = lax.all_to_all(chunks.reshape(peers, CHUNK, 1, 128), PATH, 0, 0, tiled=True)
    chunks = chunks.reshape(peers * CHUNK, 128)
    squares = kernel(
        squares_kernel,
        "sum_squares",
        out_shape=shape((shards, 128), jnp.float32),
        in_specs=[VMEM],
        out_specs=HBM,
        scratch_shapes=[pltpu.VMEM((shards, 128), jnp.float32), pltpu.SemaphoreType.DMA],
    )(chunks)
    squares = squares.reshape(shards, 1, 128)
    squares, grad = lax.optimization_barrier((squares, grad))
    squares = lax.all_to_all(squares, SHARD_ORDER, 0, 0, tiled=True)
    other = lax.ppermute(grad, "path_2", [(0, 1), (1, 0)])
    path_tiles = shape((peers, 8, 128), jnp.float32)
    *assembled, own = kernel(
        assemble_kernel,
        "assemble",
        out_shape=(path_tiles, path_tiles, shape((1, 128), jnp.float32)),
        in_specs=[VMEM] * 2,
        out_specs=(VMEM,) * 3,
        cost_estimate=pl.CostEstimate(flops=1 << 30, bytes_accessed=2 << 20, transcendentals=0),
    )(chunks, own)
    columns_grad, own = kernel(
        columns_kernel,
        "state_columns",
        out_shape=(shape(momentum.shape, jnp.float32), shape((1, 128), jnp.float32)),
        in_specs=[VMEM] * 3,
        out_specs=(VMEM,) * 2,
    )(grad, other, own)
    limit = clip_ratio * float(rows * shards * columns) ** 0.5
    update, new_momentum = kernel(
        lambda *refs: step_kernel(limit, *refs),
        "step",
        out_shape=(
            shape((peers, 8, 128), jnp.bfloat16),
            shape(momentum.shape, jnp.float32),
        ),
        in_specs=[VMEM] * 6,
        out_specs=(HBM, HBM),
        scratch_shapes=[
            pltpu.VMEM((peers, 8, 128), jnp.bfloat16),
            pltpu.VMEM(momentum.shape, jnp.float32),
            pltpu.SemaphoreType.DMA((PIECES + 1,)),
        ],
    )(
        squares.reshape(shards, 128),
        *assembled,
        columns_grad,
        own,
        momentum,
    )
    update = update.reshape(2, peers // 2, 8, 128).transpose(0, 2, 1, 3).reshape(deltas.shape)
    return (update, new_momentum)


def solution(mesh):
    finer = Mesh(
        mesh.devices.reshape(4, 8, 2, 2, 2, 2), (*PATH, *SHARD)
    )
    in_specs = (P(PATH, SHARD, None), P(None, SHARD, PATH), P())
    out_specs = (P(PATH, SHARD, None), P(None, SHARD, PATH))
    return jax.shard_map(local, mesh=finer, in_specs=in_specs, out_specs=out_specs, check_vma=False)
```

```python
import jax
import jax.numpy as jnp
from jax import lax
from jax.experimental import pallas as pl
from jax.experimental.pallas import tpu as pltpu
from jax.sharding import Mesh
from jax.sharding import PartitionSpec as P

PATH = ("path_0", "path_1", "path_2")
TILES = ("path_2", "path_0", "path_1")

SHARD = ("shard_2", "shard_1", "shard_0")
SHARD_ORDER = ("shard_1", "shard_2", "shard_0")

outer_rate = 0.7
momentum_rate = 0.9
clip_ratio = 2.0

UPPER, CHUNK = 8, 9
GRAD_BITS, LOWER_BITS = 18, 13
EXPONENTS, BIAS = 64, 128
MODULE_BITS, PACKED = 4, 8
MOMENTUM_SCALE = 8191.0
SQUARES_SCALE = 128.0
FOLD = momentum_rate * momentum_rate / (1.0 + momentum_rate)
GRAD_RATE = outer_rate * (1.0 + momentum_rate)
MOMENTUM_RATE = outer_rate * momentum_rate * momentum_rate
KERNEL_BYTES = 4 << 20
VMEM = pl.BlockSpec(memory_space=pltpu.VMEM)
SMEM = pl.BlockSpec(memory_space=pltpu.SMEM)
HBM = pl.BlockSpec(memory_space=pl.ANY)
PIECES = 4


def path_of(peer, chips):
    return (peer % chips) * 2 + peer // chips


def kernel(body, name, **kwargs):
    params = pltpu.CompilerParams(vmem_limit_bytes=KERNEL_BYTES)
    return pl.pallas_call(body, name=name, compiler_params=params, **kwargs)


def lanes():
    return lax.broadcasted_iota(jnp.int32, (8, 128), 1)


def nearest(x):
    return jnp.floor(x + 0.5).astype(jnp.int32)


def momentum_kernel(
    module_ref, mine_ref, other_ref,
    lower_ref, upper_ref, fold_ref, count_ref, peer_ref, own_ref, count,
):
    peers, modules = module_ref.shape[0], mine_ref.shape[0]
    for m in range(modules):
        count[m] = 0
    for q in range(peers):
        count[module_ref[q]] += 1
    for word in range(peers // PACKED):
        packed = 0
        for k in range(PACKED):
            m = module_ref[path_of(word * PACKED + k, peers // 2)]
            packed = packed | (m << (k * MODULE_BITS))
        peer_ref[word : word + 1, :] = jnp.full((1, 128), packed)
    chip = lax.axis_index("path_0") * lax.axis_size("path_1") + lax.axis_index("path_1")
    module = module_ref[chip * 2 + lax.axis_index("path_2")]
    own_ref[...] = (lanes()[0:1, :] == 4 * module).astype(jnp.float32)
    first_core = lax.axis_index("path_2") == 0
    row = lax.broadcasted_iota(jnp.int32, (8, 128), 0)
    for m in range(modules):
        count_ref[m : m + 1, :] = jnp.full((1, 128), count[m].astype(jnp.float32))
        mine = jnp.where(first_core, mine_ref[m, 0:8, :], mine_ref[m, 8:16, :])
        other = jnp.where(first_core, other_ref[m, 0:8, :], other_ref[m, 8:16, :])
        momentum = jnp.concatenate(
            [jnp.where(first_core, mine, other), jnp.where(first_core, other, mine)], axis=1
        )
        whole = nearest(momentum * MOMENTUM_SCALE)
        fold_ref[m] = FOLD * (momentum - whole.astype(jnp.float32) * (1.0 / MOMENTUM_SCALE))
        whole += 32768
        lower_ref[m] = whole & ((1 << LOWER_BITS) - 1)
        word = (whole >> LOWER_BITS) << (row * 3)
        for rows in (4, 2, 1):
            word = word | pltpu.roll(word, rows, 0)
        upper_ref[m : m + 1, :] = word[0:1, :]


def gather_kernel(
    column_ref, lower_ref, upper_ref, fold_ref, count_ref, peer_ref, chunk_ref, grad_ref, *scratch
):
    *sums, words = scratch
    peers, modules = column_ref.shape[0], grad_ref.shape[0]
    packed = [peer_ref[word, 0] for word in range(peers // PACKED)]
    module_of = [
        (packed[q // PACKED] >> (q % PACKED * MODULE_BITS)) & (2**MODULE_BITS - 1)
        for q in range(peers)
    ]
    for total in sums:
        total[...] = jnp.zeros_like(total)
    for q in range(peers):
        m = module_of[q]
        total = sums[q % len(sums)]
        total[m] += column_ref[q].astype(jnp.float32)
    for m in range(modules):
        total = sums[0][m]
        for more in sums[1:]:
            total += more[m]
        grad_ref[m] = total / count_ref[m : m + 1, :]
    grad = grad_ref[...]
    squares = jnp.sum(jnp.sum(grad * grad, axis=1), axis=1, keepdims=True)
    squares = nearest(squares * SQUARES_SCALE)
    row = lax.broadcasted_iota(jnp.int32, (modules, 128), 0)
    lane = lax.broadcasted_iota(jnp.int32, (modules, 128), 1)
    norms = jnp.where(lane >> 2 == row, (squares >> ((lane & 3) * 8)) & 255, 0)
    norms = jnp.sum(norms.astype(jnp.float32), axis=0, keepdims=True)
    limit = 2.0**GRAD_BITS - 1.0
    own_lane = lanes() == EXPONENTS + lax.broadcasted_iota(jnp.int32, (8, 128), 0)
    for m in range(modules):
        exact = grad_ref[m] + fold_ref[m]
        largest = jnp.max(jnp.abs(exact), axis=1, keepdims=True)
        power = jnp.ceil(jnp.log2(jnp.maximum(largest, 1e-30)))
        exact = jnp.clip(exact * jnp.exp2(GRAD_BITS - power), -limit, limit)
        words[m, 0:UPPER, :] = (nearest(exact) << LOWER_BITS) | lower_ref[m]
        powers = jnp.sum(jnp.where(own_lane, power + BIAS, 0.0), axis=0, keepdims=True)
        words[m, UPPER:CHUNK, :] = upper_ref[m : m + 1, :] | ((norms + powers).astype(jnp.int32) << 24)
    for path in range(peers):
        m = module_of[path % 2 * (peers // 2) + path // 2]
        start = path * CHUNK
        chunk_ref[start : start + UPPER, :] = words[m, 0:UPPER, :]
        chunk_ref[start + UPPER : start + CHUNK, :] = words[m, UPPER:CHUNK, :]


def squares_kernel(chunk_ref, squares_out, squares, sem):
    peers = chunk_ref.shape[0] // CHUNK
    norms = lax.shift_right_logical(chunk_ref[pl.ds(UPPER, peers, stride=CHUNK), :], 24)
    norms = jnp.sum(norms.astype(jnp.float32), axis=0, keepdims=True)
    squares[...] = jnp.broadcast_to(norms, squares.shape)
    copy = pltpu.make_async_copy(squares, squares_out, sem)
    copy.start()
    copy.wait()


def assemble_kernel(chunk_ref, own_ref, grad_ref, decay_ref, mask_ref):
    peers = grad_ref.shape[0]
    power = lax.shift_right_logical(chunk_ref[pl.ds(UPPER, peers, stride=CHUNK), :], 24)
    scale = 1.0 / jnp.exp2(GRAD_BITS + BIAS - power.astype(jnp.float32))
    row = lax.broadcasted_iota(jnp.int32, (8, 128), 0)
    own_lane = lanes() == EXPONENTS + row
    for q in range(peers):
        path = path_of(q, peers // 2)
        start = path * CHUNK
        words = chunk_ref[start : start + UPPER, :]
        of_row = jnp.where(own_lane, scale[path : path + 1, :], 0.0)
        of_row = jnp.sum(of_row, axis=1, keepdims=True) * GRAD_RATE
        grad_ref[q] = (words >> LOWER_BITS).astype(jnp.float32) * of_row
        upper = (chunk_ref[start + UPPER : start + CHUNK, :] >> (row * 3)) & 7
        whole = ((upper << LOWER_BITS) | (words & ((1 << LOWER_BITS) - 1))) - 32768
        decay_ref[q] = whole.astype(jnp.float32) * (MOMENTUM_RATE / MOMENTUM_SCALE)
    mask_ref[...] = own_ref[...]


def columns_kernel(mine_ref, other_ref, mask_ref, grad_ref, own_ref):
    core = lax.axis_index("path_2")
    for m in range(mine_ref.shape[0]):
        for half in range(2):
            grad = jnp.where(core == half, mine_ref[m], other_ref[m])
            grad = jnp.where(core == 0, grad, pltpu.roll(grad, 64, 1))
            grad_ref[m, half * 8 : half * 8 + 8, :] = grad[:, 0:64]
    own_ref[...] = mask_ref[...]


def step_kernel(
    limit, squares_ref, grad_ref, decay_ref, own_grad_ref, own_ref, momentum_ref,
    update_out, new_out, update, new, sems,
):
    peers, modules = update.shape[0], new.shape[0]
    lane = lanes()
    norm_squares = jnp.broadcast_to(jnp.sum(squares_ref[...], axis=0, keepdims=True), (8, 128))
    for byte in range(4):
        weight = 256.0**byte / SQUARES_SCALE
        norm_squares = jnp.where(lane & 3 == byte, norm_squares * weight, norm_squares)
    norm_squares += pltpu.roll(norm_squares, 127, 1)
    norm_squares = (norm_squares + pltpu.roll(norm_squares, 126, 1))[0:1, :]
    shrink = jnp.minimum(1.0, limit / jnp.sqrt(norm_squares + 1e-06))
    own = jnp.sum(jnp.where(own_ref[...] > 0.0, shrink, 0.0), axis=1, keepdims=True)
    each = peers // PIECES
    copies = []
    for piece in range(PIECES):
        tiles = slice(piece * each, (piece + 1) * each)
        step = grad_ref[tiles] * own.reshape(1, 1, 1) + decay_ref[tiles]
        update[tiles] = step.astype(jnp.bfloat16)
        copies.append(pltpu.make_async_copy(update.at[tiles], update_out.at[tiles], sems.at[piece]))
        copies[-1].start()
    for m in range(modules):
        k = jnp.sum(jnp.where(lane[0:1, :] == 4 * m, shrink, 0.0), axis=1, keepdims=True)
        new[m] = momentum_rate * momentum_ref[m] + own_grad_ref[m] * k
    copies.append(pltpu.make_async_copy(new, new_out, sems.at[PIECES]))
    copies[-1].start()
    for copy in copies:
        copy.wait()


def local(deltas, momentum, path_module):
    modules, rows, width = momentum.shape
    columns = deltas.shape[2]
    peers = lax.axis_size(PATH)
    shards = lax.axis_size(SHARD)
    shape = jax.ShapeDtypeStruct
    tiles = deltas.reshape(2, 8, peers // 2, 128).transpose(0, 2, 1, 3).reshape(peers, 8, 128)
    column_tiles = lax.all_to_all(tiles, TILES, 0, 0, tiled=True)
    other = lax.ppermute(momentum, "path_2", [(0, 1), (1, 0)])
    module_tiles = shape((modules, 8, 128), jnp.float32)
    *packed, own = kernel(
        momentum_kernel,
        "pack_momentum",
        out_shape=(
            shape((modules, 8, 128), jnp.int32),
            shape((modules, 128), jnp.int32),
            module_tiles,
            shape((modules, 128), jnp.float32),
            shape((peers // PACKED, 128), jnp.int32),
            shape((1, 128), jnp.float32),
        ),
        in_specs=[SMEM, VMEM, VMEM],
        out_specs=(VMEM,) * 6,
        scratch_shapes=[pltpu.SMEM((modules,), jnp.int32)],
    )(path_module, momentum, other)
    chunks, grad = kernel(
        gather_kernel,
        "gather_modules",
        out_shape=(shape((peers * CHUNK, 128), jnp.int32), module_tiles),
        in_specs=[VMEM] * 6,
        out_specs=(VMEM, VMEM),
        scratch_shapes=[pltpu.VMEM((modules, 8, 128), jnp.float32)] * 4
        + [pltpu.VMEM((modules, 16, 128), jnp.int32)],
    )(column_tiles, *packed)
    chunks = lax.all_to_all(chunks.reshape(peers, CHUNK, 1, 128), PATH, 0, 0, tiled=True)
    chunks = chunks.reshape(peers * CHUNK, 128)
    squares = kernel(
        squares_kernel,
        "sum_squares",
        out_shape=shape((shards, 128), jnp.float32),
        in_specs=[VMEM],
        out_specs=HBM,
        scratch_shapes=[pltpu.VMEM((shards, 128), jnp.float32), pltpu.SemaphoreType.DMA],
    )(chunks)
    squares = squares.reshape(shards, 1, 128)
    squares, grad = lax.optimization_barrier((squares, grad))
    squares = lax.all_to_all(squares, SHARD_ORDER, 0, 0, tiled=True)
    other = lax.ppermute(grad, "path_2", [(0, 1), (1, 0)])
    path_tiles = shape((peers, 8, 128), jnp.float32)
    *assembled, own = kernel(
        assemble_kernel,
        "assemble",
        out_shape=(path_tiles, path_tiles, shape((1, 128), jnp.float32)),
        in_specs=[VMEM] * 2,
        out_specs=(VMEM,) * 3,
        cost_estimate=pl.CostEstimate(flops=1 << 30, bytes_accessed=2 << 20, transcendentals=0),
    )(chunks, own)
    columns_grad, own = kernel(
        columns_kernel,
        "state_columns",
        out_shape=(shape(momentum.shape, jnp.float32), shape((1, 128), jnp.float32)),
        in_specs=[VMEM] * 3,
        out_specs=(VMEM,) * 2,
    )(grad, other, own)
    limit = clip_ratio * float(rows * shards * columns) ** 0.5
    update, new_momentum = kernel(
        lambda *refs: step_kernel(limit, *refs),
        "step",
        out_shape=(
            shape((peers, 8, 128), jnp.bfloat16),
            shape(momentum.shape, jnp.float32),
        ),
        in_specs=[VMEM] * 6,
        out_specs=(HBM, HBM),
        scratch_shapes=[
            pltpu.VMEM((peers, 8, 128), jnp.bfloat16),
            pltpu.VMEM(momentum.shape, jnp.float32),
            pltpu.SemaphoreType.DMA((PIECES + 1,)),
        ],
    )(
        squares.reshape(shards, 128),
        *assembled,
        columns_grad,
        own,
        momentum,
    )
    update = update.reshape(2, peers // 2, 8, 128).transpose(0, 2, 1, 3).reshape(deltas.shape)
    return (update, new_momentum)


def solution(mesh):
    finer = Mesh(
        mesh.devices.reshape(4, 8, 2, 2, 2, 2), (*PATH, *SHARD)
    )
    in_specs = (P(PATH, SHARD, None), P(None, SHARD, PATH), P())
    out_specs = (P(PATH, SHARD, None), P(None, SHARD, PATH))
    return jax.shard_map(local, mesh=finer, in_specs=in_specs, out_specs=out_specs, check_vma=False)
```

```python
import jax
import jax.numpy as jnp
from jax import lax
from jax.experimental import pallas as pl
from jax.experimental.pallas import tpu as pltpu
from jax.sharding import Mesh
from jax.sharding import PartitionSpec as P

PATH = ("path_0", "path_1", "path_2")
TILES = ("path_2", "path_0", "path_1")

SHARD = ("shard_2", "shard_1", "shard_0")
SHARD_ORDER = ("shard_1", "shard_2", "shard_0")

outer_rate = 0.7
momentum_rate = 0.9
clip_ratio = 2.0

UPPER, CHUNK = 8, 9
GRAD_BITS, LOWER_BITS = 18, 13
EXPONENTS, BIAS = 64, 128
MODULE_BITS, PACKED = 4, 8
MOMENTUM_SCALE = 8191.0
SQUARES_SCALE = 128.0
FOLD = momentum_rate * momentum_rate / (1.0 + momentum_rate)
KERNEL_BYTES = 4 << 20
VMEM = pl.BlockSpec(memory_space=pltpu.VMEM)
SMEM = pl.BlockSpec(memory_space=pltpu.SMEM)
HBM = pl.BlockSpec(memory_space=pl.ANY)
PIECES = 8


def path_of(peer, chips):
    return (peer % chips) * 2 + peer // chips


def kernel(body, name, **kwargs):
    params = pltpu.CompilerParams(vmem_limit_bytes=KERNEL_BYTES)
    return pl.pallas_call(body, name=name, compiler_params=params, **kwargs)


def lanes():
    return lax.broadcasted_iota(jnp.int32, (8, 128), 1)


def nearest(x):
    return jnp.floor(x + 0.5).astype(jnp.int32)


def momentum_kernel(
    module_ref, mine_ref, other_ref,
    lower_ref, upper_ref, fold_ref, count_ref, peer_ref, own_ref, count,
):
    peers, modules = module_ref.shape[0], mine_ref.shape[0]
    for m in range(modules):
        count[m] = 0
    for q in range(peers):
        count[module_ref[q]] += 1
    for word in range(peers // PACKED):
        packed = 0
        for k in range(PACKED):
            m = module_ref[path_of(word * PACKED + k, peers // 2)]
            packed = packed | (m << (k * MODULE_BITS))
        peer_ref[word : word + 1, :] = jnp.full((1, 128), packed)
    chip = lax.axis_index("path_0") * lax.axis_size("path_1") + lax.axis_index("path_1")
    module = module_ref[chip * 2 + lax.axis_index("path_2")]
    own_ref[...] = (lanes()[0:1, :] == 4 * module).astype(jnp.float32)
    first_core = lax.axis_index("path_2") == 0
    row = lax.broadcasted_iota(jnp.int32, (8, 128), 0)
    for m in range(modules):
        count_ref[m : m + 1, :] = jnp.full((1, 128), count[m].astype(jnp.float32))
        mine = jnp.where(first_core, mine_ref[m, 0:8, :], mine_ref[m, 8:16, :])
        other = jnp.where(first_core, other_ref[m, 0:8, :], other_ref[m, 8:16, :])
        momentum = jnp.concatenate(
            [jnp.where(first_core, mine, other), jnp.where(first_core, other, mine)], axis=1
        )
        whole = nearest(momentum * MOMENTUM_SCALE)
        fold_ref[m] = FOLD * (momentum - whole.astype(jnp.float32) * (1.0 / MOMENTUM_SCALE))
        whole += 32768
        lower_ref[m] = whole & ((1 << LOWER_BITS) - 1)
        word = (whole >> LOWER_BITS) << (row * 3)
        for rows in (4, 2, 1):
            word = word | pltpu.roll(word, rows, 0)
        upper_ref[m : m + 1, :] = word[0:1, :]


def gather_kernel(
    column_ref, lower_ref, upper_ref, fold_ref, count_ref, peer_ref, chunk_ref, grad_ref, *scratch
):
    *sums, words = scratch
    peers, modules = column_ref.shape[0], grad_ref.shape[0]
    packed = [peer_ref[word, 0] for word in range(peers // PACKED)]
    module_of = [
        (packed[q // PACKED] >> (q % PACKED * MODULE_BITS)) & (2**MODULE_BITS - 1)
        for q in range(peers)
    ]
    for total in sums:
        total[...] = jnp.zeros_like(total)
    for q in range(peers):
        m = module_of[q]
        total = sums[q % len(sums)]
        total[m] += column_ref[q].astype(jnp.float32)
    for m in range(modules):
        total = sums[0][m]
        for more in sums[1:]:
            total += more[m]
        grad_ref[m] = total / count_ref[m : m + 1, :]
    grad = grad_ref[...]
    squares = jnp.sum(jnp.sum(grad * grad, axis=1), axis=1, keepdims=True)
    squares = nearest(squares * SQUARES_SCALE)
    row = lax.broadcasted_iota(jnp.int32, (modules, 128), 0)
    lane = lax.broadcasted_iota(jnp.int32, (modules, 128), 1)
    norms = jnp.where(lane >> 2 == row, (squares >> ((lane & 3) * 8)) & 255, 0)
    norms = jnp.sum(norms.astype(jnp.float32), axis=0, keepdims=True)
    limit = 2.0**GRAD_BITS - 1.0
    own_lane = lanes() == EXPONENTS + lax.broadcasted_iota(jnp.int32, (8, 128), 0)
    for m in range(modules):
        exact = grad_ref[m] + fold_ref[m]
        largest = jnp.max(jnp.abs(exact), axis=1, keepdims=True)
        power = jnp.ceil(jnp.log2(jnp.maximum(largest, 1e-30)))
        exact = jnp.clip(exact * jnp.exp2(GRAD_BITS - power), -limit, limit)
        words[m, 0:UPPER, :] = (nearest(exact) << LOWER_BITS) | lower_ref[m]
        powers = jnp.sum(jnp.where(own_lane, power + BIAS, 0.0), axis=0, keepdims=True)
        words[m, UPPER:CHUNK, :] = upper_ref[m : m + 1, :] | ((norms + powers).astype(jnp.int32) << 24)
    for path in range(peers):
        m = module_of[path % 2 * (peers // 2) + path // 2]
        start = path * CHUNK
        chunk_ref[start : start + UPPER, :] = words[m, 0:UPPER, :]
        chunk_ref[start + UPPER : start + CHUNK, :] = words[m, UPPER:CHUNK, :]


def squares_kernel(chunk_ref, squares_out, squares, sem):
    peers = chunk_ref.shape[0] // CHUNK
    norms = lax.shift_right_logical(chunk_ref[pl.ds(UPPER, peers, stride=CHUNK), :], 24)
    norms = jnp.sum(norms.astype(jnp.float32), axis=0, keepdims=True)
    squares[...] = jnp.broadcast_to(norms, squares.shape)
    copy = pltpu.make_async_copy(squares, squares_out, sem)
    copy.start()
    copy.wait()


def assemble_kernel(chunk_ref, own_ref, grad_ref, decay_ref, mask_ref):
    peers = grad_ref.shape[0]
    power = lax.shift_right_logical(chunk_ref[pl.ds(UPPER, peers, stride=CHUNK), :], 24)
    scale = 1.0 / jnp.exp2(GRAD_BITS + BIAS - power.astype(jnp.float32))
    row = lax.broadcasted_iota(jnp.int32, (8, 128), 0)
    own_lane = lanes() == EXPONENTS + row
    for q in range(peers):
        path = path_of(q, peers // 2)
        start = path * CHUNK
        words = chunk_ref[start : start + UPPER, :]
        of_row = jnp.where(own_lane, scale[path : path + 1, :], 0.0)
        of_row = jnp.sum(of_row, axis=1, keepdims=True)
        grad_ref[q] = (words >> LOWER_BITS).astype(jnp.float32) * of_row
        upper = (chunk_ref[start + UPPER : start + CHUNK, :] >> (row * 3)) & 7
        whole = ((upper << LOWER_BITS) | (words & ((1 << LOWER_BITS) - 1))) - 32768
        decay_ref[q] = whole.astype(jnp.float32) * (momentum_rate / MOMENTUM_SCALE)
    mask_ref[...] = own_ref[...]


def columns_kernel(mine_ref, other_ref, mask_ref, grad_ref, own_ref):
    core = lax.axis_index("path_2")
    for m in range(mine_ref.shape[0]):
        for half in range(2):
            grad = jnp.where(core == half, mine_ref[m], other_ref[m])
            grad = jnp.where(core == 0, grad, pltpu.roll(grad, 64, 1))
            grad_ref[m, half * 8 : half * 8 + 8, :] = grad[:, 0:64]
    own_ref[...] = mask_ref[...]


def step_kernel(
    limit, squares_ref, grad_ref, decay_ref, own_grad_ref, own_ref, momentum_ref,
    update_out, new_out, update, new, sems,
):
    peers, modules = update.shape[0], new.shape[0]
    lane = lanes()
    norm_squares = jnp.broadcast_to(jnp.sum(squares_ref[...], axis=0, keepdims=True), (8, 128))
    for byte in range(4):
        weight = 256.0**byte / SQUARES_SCALE
        norm_squares = jnp.where(lane & 3 == byte, norm_squares * weight, norm_squares)
    norm_squares += pltpu.roll(norm_squares, 127, 1)
    norm_squares = (norm_squares + pltpu.roll(norm_squares, 126, 1))[0:1, :]
    shrink = jnp.minimum(1.0, limit / jnp.sqrt(norm_squares + 1e-06))
    own = jnp.sum(jnp.where(own_ref[...] > 0.0, shrink, 0.0), axis=1, keepdims=True)
    each = peers // PIECES
    copies = []
    for piece in range(PIECES):
        tiles = slice(piece * each, (piece + 1) * each)
        clipped = grad_ref[tiles] * own.reshape(1, 1, 1)
        step = outer_rate * (clipped + momentum_rate * (decay_ref[tiles] + clipped))
        update[tiles] = step.astype(jnp.bfloat16)
        copies.append(pltpu.make_async_copy(update.at[tiles], update_out.at[tiles], sems.at[piece]))
        copies[-1].start()
    for m in range(modules):
        k = jnp.sum(jnp.where(lane[0:1, :] == 4 * m, shrink, 0.0), axis=1, keepdims=True)
        new[m] = momentum_rate * momentum_ref[m] + own_grad_ref[m] * k
    copies.append(pltpu.make_async_copy(new, new_out, sems.at[PIECES]))
    copies[-1].start()
    for copy in copies:
        copy.wait()


def local(deltas, momentum, path_module):
    modules, rows, width = momentum.shape
    columns = deltas.shape[2]
    peers = lax.axis_size(PATH)
    shards = lax.axis_size(SHARD)
    shape = jax.ShapeDtypeStruct
    tiles = deltas.reshape(2, 8, peers // 2, 128).transpose(0, 2, 1, 3).reshape(peers, 8, 128)
    column_tiles = lax.all_to_all(tiles, TILES, 0, 0, tiled=True)
    other = lax.ppermute(momentum, "path_2", [(0, 1), (1, 0)])
    module_tiles = shape((modules, 8, 128), jnp.float32)
    *packed, own = kernel(
        momentum_kernel,
        "pack_momentum",
        out_shape=(
            shape((modules, 8, 128), jnp.int32),
            shape((modules, 128), jnp.int32),
            module_tiles,
            shape((modules, 128), jnp.float32),
            shape((peers // PACKED, 128), jnp.int32),
            shape((1, 128), jnp.float32),
        ),
        in_specs=[SMEM, VMEM, VMEM],
        out_specs=(VMEM,) * 6,
        scratch_shapes=[pltpu.SMEM((modules,), jnp.int32)],
    )(path_module, momentum, other)
    chunks, grad = kernel(
        gather_kernel,
        "gather_modules",
        out_shape=(shape((peers * CHUNK, 128), jnp.int32), module_tiles),
        in_specs=[VMEM] * 6,
        out_specs=(VMEM, VMEM),
        scratch_shapes=[pltpu.VMEM((modules, 8, 128), jnp.float32)] * 4
        + [pltpu.VMEM((modules, 16, 128), jnp.int32)],
    )(column_tiles, *packed)
    chunks = lax.all_to_all(chunks.reshape(peers, CHUNK, 1, 128), PATH, 0, 0, tiled=True)
    chunks = chunks.reshape(peers * CHUNK, 128)
    squares = kernel(
        squares_kernel,
        "sum_squares",
        out_shape=shape((shards, 128), jnp.float32),
        in_specs=[VMEM],
        out_specs=HBM,
        scratch_shapes=[pltpu.VMEM((shards, 128), jnp.float32), pltpu.SemaphoreType.DMA],
    )(chunks)
    squares = squares.reshape(shards, 1, 128)
    squares, grad = lax.optimization_barrier((squares, grad))
    squares = lax.all_to_all(squares, SHARD_ORDER, 0, 0, tiled=True)
    other = lax.ppermute(grad, "path_2", [(0, 1), (1, 0)])
    path_tiles = shape((peers, 8, 128), jnp.float32)
    *assembled, own = kernel(
        assemble_kernel,
        "assemble",
        out_shape=(path_tiles, path_tiles, shape((1, 128), jnp.float32)),
        in_specs=[VMEM] * 2,
        out_specs=(VMEM,) * 3,
        cost_estimate=pl.CostEstimate(flops=1 << 30, bytes_accessed=2 << 20, transcendentals=0),
    )(chunks, own)
    columns_grad, own = kernel(
        columns_kernel,
        "state_columns",
        out_shape=(shape(momentum.shape, jnp.float32), shape((1, 128), jnp.float32)),
        in_specs=[VMEM] * 3,
        out_specs=(VMEM,) * 2,
    )(grad, other, own)
    limit = clip_ratio * float(rows * shards * columns) ** 0.5
    update, new_momentum = kernel(
        lambda *refs: step_kernel(limit, *refs),
        "step",
        out_shape=(
            shape((peers, 8, 128), jnp.bfloat16),
            shape(momentum.shape, jnp.float32),
        ),
        in_specs=[VMEM] * 6,
        out_specs=(HBM, HBM),
        scratch_shapes=[
            pltpu.VMEM((peers, 8, 128), jnp.bfloat16),
            pltpu.VMEM(momentum.shape, jnp.float32),
            pltpu.SemaphoreType.DMA((PIECES + 1,)),
        ],
    )(
        squares.reshape(shards, 128),
        *assembled,
        columns_grad,
        own,
        momentum,
    )
    update = update.reshape(2, peers // 2, 8, 128).transpose(0, 2, 1, 3).reshape(deltas.shape)
    return (update, new_momentum)


def solution(mesh):
    finer = Mesh(
        mesh.devices.reshape(4, 8, 2, 2, 2, 2), (*PATH, *SHARD)
    )
    in_specs = (P(PATH, SHARD, None), P(None, SHARD, PATH), P())
    out_specs = (P(PATH, SHARD, None), P(None, SHARD, PATH))
    return jax.shard_map(local, mesh=finer, in_specs=in_specs, out_specs=out_specs, check_vma=False)
```
